32 devices in a mesh: pool: 4 (over y, x), dev: 8 (over z, core).
Axes of the slice: x: 2, y: 2, z: 4, core: 2. Of those that a mesh axis runs over, the one named last changes fastest.
Arguments:
- latent: bfloat16 [4, 4, 16, 32768], P('pool', None, None, 'dev'), may hold values from -6 to 6
- tile_routes: int32 [4, 8, 4, 1], P('pool', 'dev'), may hold values from 0 to 4; in each aligned block of 4 rows (0 to 3, 4 to 7, ..., all dimensions but the last counted through in order) no two rows name the same one
- w_in: bfloat16 [4, 3, 3, 16, 128], P('pool'), may hold values from -0.5 to 0.5
- w_qkv: bfloat16 [4, 128, 384], P('pool'), may hold values from -0.5 to 0.5
- w_proj: bfloat16 [4, 128, 128], P('pool'), may hold values from -0.5 to 0.5
- w_mid: bfloat16 [4, 3, 3, 128, 128], P('pool'), may hold values from -0.1875 to 0.1875
- w_up: bfloat16 [4, 128, 512], P('pool'), may hold values from -0.5 to 0.5
- w_down: bfloat16 [4, 512, 128], P('pool'), may hold values from -0.25 to 0.25
- w_out: bfloat16 [4, 3, 3, 128, 16], P('pool'), may hold values from -0.1875 to 0.1875
- dec_in: bfloat16 [3, 3, 3, 16, 192], replicated, may hold values from -0.3125 to 0.3125
- dec_mid: bfloat16 [3, 3, 192, 192], replicated, may hold values from -0.15625 to 0.15625
Outputs:
- decoded: bfloat16 [4, 4, 192, 64, 512], P('pool', None, None, 'dev')
The draws below stay inside these ranges and needn't reach their ends.
Inputs may be any that keep to these rules, and one draw needn't show every extreme that they name: `tile_routes`: the value 4 marks a tile without detail; a smaller value names the refiner group. Among the 4 tiles of one device no value appears more than 1 times, and in every draw some device has one value exactly 1 times.
All inputs are finite; a program needn't handle non-finite values.
Results may differ from the reference program's by a relative error of at most 0.01.
Values may be sent and summed in bfloat16 or wider, within the bound.
No kernel may reach another device: no remote copies, remote signals or barrier semaphores. Data moves between devices by JAX's collectives and lax.ppermute only.
A program may use at most 640 MiB of HBM per device.

```python
import math
import jax
import jax.numpy as jnp
import numpy as np
from jax import lax

C = 16
HID = 128
HEAD = 64
MLP = 512
DEC = 192
TILE = 64
WIN = 8
FRAMES = 4
CAPG = 1
CELLS = 32768
N_POOL = 4
N_DEV = 8


def block_levels(own_key, dims, pieces, low, top_value):
    loudness = 1.0
    for position, shards_of in pieces:
        steps = jax.random.uniform(jax.random.fold_in(jax.random.fold_in(own_key, 6), position), (shards_of,), jnp.float32, low / len(pieces), top_value / len(pieces))
        loudness = loudness * jnp.repeat(jnp.exp(steps), dims[position] // shards_of).reshape((-1,) + (1,) * (len(dims) - 1 - position))
    return loudness


def routed_block(own_key, own, number, rows, count, top, limit, slope):
    sequence = jax.random.permutation(own_key, count)
    crowded, usual = portions_of(count, rows * top, limit, slope, True), portions_of(count, rows * top, limit, slope, False)
    places = jnp.arange(count)

    def named(tallies, offset_by):
        used = int((tallies > 0).sum())
        fixed = max(1, used // 4)
        moved = fixed + (places - fixed + offset_by * (used - fixed)) % max(1, count - fixed)
        return jnp.zeros((count,), jnp.int32).at[sequence[jnp.where(places < fixed, places, moved)]].set(jnp.asarray(tallies, jnp.int32))

    tallies = jnp.where(number % 4 == 0, named(crowded, number // 4), named(usual, number - number // 4 - 1))
    mixed = jax.random.permutation(jax.random.fold_in(own, 3), count)
    giver, sink = mixed[0:count // 2 * 2:2], mixed[1:count // 2 * 2:2]
    margin = jnp.minimum(tallies[giver] - 1, limit - tallies[sink]) // 2
    margin = jnp.where((giver == sequence[0]) | (sink == sequence[0]) | (tallies[sink] == 0), 0, jnp.maximum(margin, 0))
    moved = jax.random.randint(jax.random.fold_in(own, 4), (count // 2,), 0, 1 << 20) % (margin + 1)
    tallies = tallies.at[giver].add(-moved).at[sink].add(moved)
    items = jnp.searchsorted(jnp.cumsum(tallies), jnp.arange(rows * top), side="right").astype(jnp.int32)
    grid = items.reshape(top, rows).T
    grid = grid[jax.random.permutation(jax.random.fold_in(own, 1), rows)]
    offset_by = jax.random.randint(jax.random.fold_in(own, 2), (rows, 1), 0, top)
    return jnp.take_along_axis(grid, (jnp.arange(top)[None, :] + offset_by) % top, axis=1)


def portions_of(amount, total, limit, skew, full):
    weights = [(1 << 20) // math.isqrt(grade ** skew) + 1 for grade in range(1, amount + 1)]
    largest = limit if full else min(limit, max(-(-total // amount), total * weights[0] // sum(weights)))
    least = 1 if total - largest >= amount - 1 else 0
    given, rest = [largest] + [least] * (amount - 1), total - largest - least * (amount - 1)
    while rest > 0:
        candidates = [i for i in range(1, amount) if given[i] < largest] or [i for i in range(1, amount) if given[i] < limit]
        mass, left = sum([weights[i] for i in candidates]), rest
        for i in candidates:
            extra = min(limit - given[i], max(1, left * weights[i] // mass), rest)
            given[i] = given[i] + extra
            rest = rest - extra
    return np.array(given)


def scatter_about(stream_key, dims, deviation, most, shards=(), held_as=jnp.bfloat16):
    array = jax.random.normal(stream_key, dims, jnp.float32) * deviation
    if len(shards) > 0:
        array = block_levels(stream_key, dims, shards, -0.22, 0.18) * array
    return jnp.clip(array, min=-most, max=most).astype(held_as)


def setup_inputs(seed: int = 0) -> dict:
    key_list = jax.random.split(jax.random.key(seed), 12)
    latent = scatter_about(key_list[0], (N_POOL, FRAMES, C, CELLS), 1.0, 6.0, ((0, 4), (3, 8)))
    tile_routes_keys = jax.random.split(jax.random.fold_in(key_list[1], 1), N_POOL * N_DEV * FRAMES // FRAMES)
    tile_routes_turns = jax.random.permutation(jax.random.fold_in(key_list[1], 3), N_POOL * N_DEV * FRAMES // FRAMES)
    tile_routes = jax.vmap(lambda own, number: routed_block(jax.random.fold_in(key_list[1], 2), own, number, FRAMES, N_POOL + 1, 1, CAPG, 2))(tile_routes_keys, tile_routes_turns).reshape((N_POOL, N_DEV, FRAMES, 1))
    w_in = scatter_about(key_list[2], (N_POOL, 3, 3, C, HID), (9 * C) ** -0.5, 0.5, ((0, 4),))
    w_qkv = scatter_about(key_list[3], (N_POOL, HID, 3 * HID), HID ** -0.5, 0.5, ((0, 4),))
    w_proj = scatter_about(key_list[4], (N_POOL, HID, HID), HID ** -0.5, 0.5, ((0, 4),))
    w_mid = scatter_about(key_list[5], (N_POOL, 3, 3, HID, HID), (9 * HID) ** -0.5, 0.1875, ((0, 4),))
    w_up = scatter_about(key_list[6], (N_POOL, HID, MLP), HID ** -0.5, 0.5, ((0, 4),))
    w_down = scatter_about(key_list[7], (N_POOL, MLP, HID), MLP ** -0.5, 0.25, ((0, 4),))
    w_out = scatter_about(key_list[8], (N_POOL, 3, 3, HID, C), (9 * HID) ** -0.5, 0.1875, ((0, 4),))
    dec_in = scatter_about(key_list[9], (3, 3, 3, C, DEC), (27 * C) ** -0.5, 0.3125)
    dec_mid = scatter_about(key_list[10], (3, 3, DEC, DEC), (9 * DEC) ** -0.5, 0.15625)
    return {"latent": latent, "tile_routes": tile_routes, "w_in": w_in, "w_qkv": w_qkv, "w_proj": w_proj, "w_mid": w_mid, "w_up": w_up, "w_down": w_down, "w_out": w_out, "dec_in": dec_in, "dec_mid": dec_mid}


epsilon = 1e-06

def normalize(values):
    return values * lax.rsqrt(lax.optimization_barrier(jnp.mean(values * values, axis=-1, keepdims=True)) + epsilon)

def conv_grid(tile_grid, weight):
    tile_side = tile_grid.shape[0]
    padded = jnp.pad(tile_grid, ((1, 1), (1, 1), (0, 0)))
    shifted = [padded[shift_y:shift_y + tile_side, shift_x:shift_x + tile_side, :] for shift_y in range(3) for shift_x in range(3)]
    stacked = jnp.concatenate(shifted, axis=2).reshape(tile_side * tile_side, -1)
    return jnp.dot(stacked, weight.reshape(-1, weight.shape[3]), preferred_element_type=jnp.float32)

def window_attention(normed, w_qkv, w_proj, tile_side):
    channels = normed.shape[1]
    head_count = channels // HEAD
    per_side = tile_side // WIN
    mixed = jnp.dot(normed, w_qkv, preferred_element_type=jnp.float32).astype(jnp.bfloat16)
    mixed = mixed.reshape(per_side, WIN, per_side, WIN, 3, head_count, HEAD).transpose(0, 2, 4, 5, 1, 3, 6)
    mixed = mixed.reshape(per_side * per_side, 3, head_count, WIN * WIN, HEAD)
    queries = mixed[:, 0].astype(jnp.float32)
    key_block = mixed[:, 1].astype(jnp.float32)
    value_block = mixed[:, 2].astype(jnp.float32)
    scores = jnp.einsum('nhld,nhmd->nhlm', queries, key_block) / math.sqrt(HEAD)
    top_score = lax.optimization_barrier(jnp.max(scores, axis=-1, keepdims=True))
    raised = jnp.exp(scores - top_score)
    attn_weights = (raised / lax.optimization_barrier(jnp.sum(raised, axis=-1, keepdims=True))).astype(jnp.bfloat16)
    attended = jnp.einsum('nhlm,nhmd->nhld', attn_weights.astype(jnp.float32), value_block).astype(jnp.bfloat16)
    attended = attended.reshape(per_side, per_side, head_count, WIN, WIN, HEAD).transpose(0, 3, 1, 4, 2, 5)
    attended = attended.reshape(tile_side * tile_side, channels)
    return jnp.dot(attended, w_proj, preferred_element_type=jnp.float32)

def refine_tile(one_tile, weights):
    w_in, w_qkv, w_proj, w_mid, w_up, w_down, w_out = weights
    latent_ch, tile_cells = one_tile.shape
    tile_side = math.isqrt(tile_cells)
    tile_grid = one_tile.reshape(latent_ch, tile_side, tile_side).transpose(1, 2, 0)
    lifted = conv_grid(tile_grid, w_in)
    channels = lifted.shape[1]
    attended = lifted + window_attention(normalize(lifted).astype(jnp.bfloat16), w_qkv, w_proj, tile_side)
    conv_input = normalize(attended).astype(jnp.bfloat16).reshape(tile_side, tile_side, channels)
    convolved = attended + jax.nn.silu(conv_grid(conv_input, w_mid))
    mlp_input = normalize(convolved).astype(jnp.bfloat16)
    expanded = jax.nn.silu(jnp.dot(mlp_input, w_up, preferred_element_type=jnp.float32)).astype(jnp.bfloat16)
    finished = convolved + jnp.dot(expanded, w_down, preferred_element_type=jnp.float32)
    out_grid = finished.astype(jnp.bfloat16).reshape(tile_side, tile_side, channels)
    return conv_grid(out_grid, w_out).astype(jnp.bfloat16).T

def causal_conv(row_padded, weight):
    frames, latent_ch, row_total, col_total = row_padded.shape
    out_rows = row_total - 2
    padded = jnp.pad(row_padded, ((2, 0), (0, 0), (0, 0), (1, 1))).astype(jnp.float32)
    summed = jnp.zeros((frames, weight.shape[4], out_rows, col_total), jnp.float32)
    for shift_t in range(3):
        for shift_y in range(3):
            for shift_x in range(3):
                piece = padded[shift_t:shift_t + frames, :, shift_y:shift_y + out_rows, shift_x:shift_x + col_total]
                summed = summed + jnp.einsum('fcrw,cd->fdrw', piece, weight[shift_t, shift_y, shift_x].astype(jnp.float32))
    return summed

def strip_conv(row_padded, weight):
    frames, channels, row_total, col_total = row_padded.shape
    out_rows = row_total - 2
    padded = jnp.pad(row_padded, ((0, 0), (0, 0), (0, 0), (1, 1))).astype(jnp.float32)
    summed = jnp.zeros((frames, weight.shape[3], out_rows, col_total), jnp.float32)
    for shift_y in range(3):
        for shift_x in range(3):
            piece = padded[:, :, shift_y:shift_y + out_rows, shift_x:shift_x + col_total]
            summed = summed + jnp.einsum('fcrw,cd->fdrw', piece, weight[shift_y, shift_x].astype(jnp.float32))
    return summed

def decode_strip(strip, dec_in, dec_mid):
    row_padded = jnp.pad(strip, ((0, 0), (0, 0), (1, 1), (0, 0)))
    activation = jax.nn.silu(causal_conv(row_padded, dec_in)).astype(jnp.bfloat16)
    act_padded = jnp.pad(activation, ((0, 0), (0, 0), (1, 1), (0, 0)))
    return (activation.astype(jnp.float32) + strip_conv(act_padded, dec_mid)).astype(jnp.bfloat16)

def reference(latent, tile_routes, w_in, w_qkv, w_proj, w_mid, w_up, w_down, w_out, dec_in, dec_mid):
    tile_cells = TILE * TILE
    own_tiles = latent.reshape(N_POOL, FRAMES, C, N_DEV, tile_cells).transpose(0, 3, 1, 2, 4)
    own_tiles = own_tiles.reshape(N_POOL * N_DEV * FRAMES, C, tile_cells)
    destination = tile_routes.reshape(-1)
    stacked_weights = (w_in, w_qkv, w_proj, w_mid, w_up, w_down, w_out)

    def refine_one(packed):
        one_tile, target = packed
        chosen = jnp.minimum(target, N_POOL - 1)
        weights = tuple((lax.dynamic_index_in_dim(weight, chosen, 0, keepdims=False) for weight in stacked_weights))
        tile_delta = refine_tile(one_tile, weights)
        return jnp.where(target < N_POOL, tile_delta, jnp.zeros_like(tile_delta))
    deltas = lax.map(refine_one, (own_tiles, destination))
    blended = (own_tiles.astype(jnp.float32) + deltas.astype(jnp.float32)).astype(jnp.bfloat16)
    strips = blended.reshape(N_POOL, N_DEV, FRAMES, C, TILE, TILE).transpose(0, 2, 3, 4, 1, 5)
    strips = strips.reshape(N_POOL, FRAMES, C, TILE, N_DEV * TILE)
    return lax.map(lambda strip: decode_strip(strip, dec_in, dec_mid), strips)
```

```python
import functools
import math

import jax
import jax.numpy as jnp
from jax import lax
from jax.experimental import pallas as pl
from jax.experimental.pallas import tpu as pltpu
from jax.sharding import PartitionSpec as P

HEAD = 64
WIN = 8
LANES = 128
META = 8
EPS = 1e-06
F32 = jnp.float32
BF16 = jnp.bfloat16
VMEM_LIMIT = 60 * 2**20


def dot(a, b):
    return jnp.dot(a, b, preferred_element_type=F32)


def dot_tn(a, b):
    return lax.dot_general(a, b, (((0,), (0,)), ((), ())), preferred_element_type=F32)


def silu(x):
    half = 0.5 * x
    return half + half * jnp.tanh(half)


def norm_channels(x):
    mean = jnp.mean(x * x, axis=0, keepdims=True)
    return x * lax.rsqrt(mean + EPS)


def lane_iota(width):
    return lax.broadcasted_iota(jnp.int32, (1, width), 1)


def frame_of(group, groups, routes_ref):
    frames = groups
    named = functools.reduce(jnp.logical_or, [routes_ref[f] == group for f in range(frames)])
    wanted = jnp.where(named, group, groups)
    return sum(jnp.where(routes_ref[f] == wanted, f, 0) for f in range(frames)), named


def pick_kernel(routes_ref, tile_ref, out_ref):
    groups = pl.num_programs(0)
    group = pl.program_id(0)
    n_groups = out_ref.shape[0] * 0 + routes_ref.shape[0]
    frame, named = frame_of(group, n_groups, routes_ref)
    ch, cells = tile_ref.shape[1:]
    out_ref[0, :, :cells] = tile_ref[0]
    rows = lax.broadcasted_iota(jnp.int32, (ch, LANES), 0)
    live = jnp.where(named, 1, 0)
    out_ref[0, :, cells:] = jnp.where(rows < META, frame, live).astype(F32).astype(BF16)


def pick_tiles(routes, own_tiles, groups):
    frames, ch, cells = own_tiles.shape
    assert frames == groups
    return pl.pallas_call(
        pick_kernel,
        out_shape=jax.ShapeDtypeStruct((groups, ch, cells + LANES), BF16),
        grid_spec=pltpu.PrefetchScalarGridSpec(
            num_scalar_prefetch=1,
            grid=(groups,),
            in_specs=[
                pl.BlockSpec(
                    (1, ch, cells), lambda g, r: (frame_of(g, groups, r)[0], 0, 0)
                )
            ],
            out_specs=pl.BlockSpec((1, ch, cells + LANES), lambda g, r: (g, 0, 0)),
        ),
        name="pick",
    )(routes, own_tiles)


def refine_kernel(
    tile_ref, w_in, w_qkv, w_proj, w_mid, w_up, w_down, w_out, out_ref,
    t_in, t_qkv, t_proj, t_mid, t_up, t_down, perm, patch, att, even, odd, taps, padded,
    *, side, bands,
):
    ch = tile_ref.shape[1]
    cells = side * side
    hid = w_proj.shape[0]
    chunk = WIN * side
    chunks = cells // chunk
    heads = hid // HEAD
    win_cells = WIN * WIN
    pair = LANES // win_cells
    assert side == WIN * WIN and pair == 2 and 2 * side == LANES

    @pl.when(pl.program_id(0) == 0)
    def _():
        t_in[...] = w_in[...].astype(F32).T.astype(BF16)
        t_qkv[...] = w_qkv[...].astype(F32).T.astype(BF16)
        t_proj[...] = w_proj[...].astype(F32).T.astype(BF16)
        t_mid[...] = w_mid[...].astype(F32).T.astype(BF16)
        t_up[...] = w_up[...].astype(F32).T.astype(BF16)
        t_down[...] = w_down[...].astype(F32).T.astype(BF16)
        src = lax.broadcasted_iota(jnp.int32, (chunk, chunk), 0)
        dst = lax.broadcasted_iota(jnp.int32, (chunk, chunk), 1)
        want = ((dst >> 3) & 7) * side + (dst >> 6) * WIN + (dst & 7)
        perm[...] = jnp.where(src == want, 1.0, 0.0).astype(BF16)
        even[:, :LANES] = jnp.zeros((3 * hid, LANES), BF16)
        even[:, LANES + cells :] = jnp.zeros((3 * hid, LANES), BF16)
        padded[:, :LANES] = jnp.zeros((ch, LANES), BF16)
        padded[:, LANES + cells :] = jnp.zeros((ch, LANES), BF16)

    tile = tile_ref[0, :, :cells].astype(F32)
    lane = lane_iota(cells)
    row = lane >> 6
    col = lane & (side - 1)

    def inside(dy, dx):
        ok = None
        for pos, off in ((row, dy), (col, dx)):
            if off:
                good = (pos > 0) if off < 0 else (pos < side - 1)
                ok = good if ok is None else ok & good
        return ok

    def moved(x, dy, dx):
        off = dy * side + dx
        if off == 0:
            return x
        x = pltpu.roll(x, (-off) % cells, 1)
        return jnp.where(inside(dy, dx), x, 0.0)

    offsets = [(dy, dx) for dy in (-1, 0, 1) for dx in (-1, 0, 1)]
    for t, (dy, dx) in enumerate(offsets):
        patch[t * ch : (t + 1) * ch, :] = moved(tile, dy, dx).astype(BF16)

    low = lane_iota(LANES) < win_cells
    ccol = lane_iota(chunk) & (side - 1)
    scale = math.log2(math.e) / math.sqrt(HEAD)

    def attend(c, _):
        base = pl.multiple_of(c * chunk, chunk)
        lifted = dot(t_in[...], patch[:, pl.ds(base, chunk)])
        normed = norm_channels(lifted).astype(BF16)
        windows = dot(normed, perm[...]).astype(BF16)
        qkv = dot(t_qkv[...], windows).astype(BF16)
        mixed = []
        for h in range(heads):
            parts = []
            for p in range(chunk // LANES):
                def piece(kind):
                    top = kind * hid + h * HEAD
                    return qkv[top : top + HEAD, p * LANES : (p + 1) * LANES]
                scores = dot_tn(piece(1), piece(0))
                scores = jnp.where(low, scores[:win_cells], scores[win_cells:])
                top = jnp.max(scores, axis=0, keepdims=True)
                raised = jnp.exp2((scores - top) * scale)
                total = jnp.sum(raised, axis=0, keepdims=True)
                probs = raised * (1.0 / total)
                spread = jnp.concatenate(
                    [jnp.where(low, probs, 0.0), jnp.where(low, 0.0, probs)], axis=0
                ).astype(BF16)
                parts.append(dot(piece(2), spread))
            mixed.append(jnp.concatenate(parts, axis=1))
        mixed = jnp.concatenate(mixed, axis=0).astype(BF16)
        mixed = dot(mixed, perm[...]).astype(BF16)
        attended = lifted + dot(t_proj[...], mixed)
        att[:, pl.ds(base, chunk)] = attended
        conv_in = norm_channels(attended)
        left = jnp.where(ccol > 0, pltpu.roll(conv_in, 1, 1), 0.0)
        right = jnp.where(ccol < side - 1, pltpu.roll(conv_in, chunk - 1, 1), 0.0)
        here = pl.ds(pl.multiple_of(base + LANES, LANES), chunk)
        even[:hid, here] = left.astype(BF16)
        even[hid : 2 * hid, here] = conv_in.astype(BF16)
        even[2 * hid :, here] = right.astype(BF16)
        around = even[:, pl.ds(base, chunk + LANES)]
        odd[:, pl.ds(base, chunk)] = around[:, side : side + chunk]
        return 0

    lax.fori_loop(0, chunks, attend, 0)
    odd[:, cells:] = even[:, cells : cells + 2 * LANES][:, side : side + LANES]

    def finish(c, _):
        base = pl.multiple_of(c * chunk, chunk)
        after = pl.ds(pl.multiple_of(base + LANES, LANES), chunk)
        around = jnp.concatenate(
            [odd[:, pl.ds(base, chunk)], even[:, after], odd[:, after]], axis=0
        )
        convolved = att[:, pl.ds(base, chunk)] + silu(dot(t_mid[...], around))
        mlp_in = norm_channels(convolved).astype(BF16)
        expanded = silu(dot(t_up[...], mlp_in)).astype(BF16)
        finished = convolved + dot(t_down[...], expanded)
        taps[:, pl.ds(base, chunk)] = dot(w_out[...], finished.astype(BF16))
        return 0

    lax.fori_loop(0, chunks, finish, 0)

    delta = jnp.zeros((ch, cells), F32)
    for t, (dy, dx) in enumerate(offsets):
        delta = delta + moved(taps[t * ch : (t + 1) * ch, :], dy, dx)
    delta = delta.astype(BF16).astype(F32)
    note = tile_ref[0, :, cells:]
    live = note[META : META + 1, :1].astype(F32)
    padded[:, LANES : LANES + cells] = (tile + live * delta).astype(BF16)
    band = cells // bands
    pieces = (band + 2 * LANES) // LANES
    for b in range(bands):
        for j in range(pieces):
            at = b * band + j * LANES
            out_ref[b, j * ch : (j + 1) * ch, :] = padded[:, at : at + LANES]
        out_ref[b, pieces * ch :, :] = note[:META, :]


def refine_tiles(tiles, weights, bands):
    count, ch, width = tiles.shape
    cells = width - LANES
    side = math.isqrt(cells)
    w_in, w_qkv, w_proj, w_mid, w_up, w_down, w_out = weights
    hid = w_proj.shape[0]
    mlp = w_up.shape[1]
    w_in = w_in.reshape(-1, hid)
    w_mid = w_mid.reshape(-1, hid)
    w_out = jnp.swapaxes(w_out, 2, 3).reshape(-1, hid)
    taps = w_out.shape[0]
    chunk = WIN * side
    rows = (cells // bands + 2 * LANES) // LANES * ch + META
    whole = pl.BlockSpec(memory_space=pltpu.VMEM)
    return pl.pallas_call(
        functools.partial(refine_kernel, side=side, bands=bands),
        out_shape=jax.ShapeDtypeStruct((count * bands, rows, LANES), BF16),
        grid=(count,),
        in_specs=[pl.BlockSpec((1, ch, width), lambda i: (i, 0, 0))] + [whole] * 7,
        out_specs=pl.BlockSpec((bands, rows, LANES), lambda i: (i, 0, 0)),
        scratch_shapes=[
            pltpu.VMEM((hid, w_in.shape[0]), BF16),
            pltpu.VMEM((3 * hid, hid), BF16),
            pltpu.VMEM((hid, hid), BF16),
            pltpu.VMEM((hid, w_mid.shape[0]), BF16),
            pltpu.VMEM((mlp, hid), BF16),
            pltpu.VMEM((hid, mlp), BF16),
            pltpu.VMEM((chunk, chunk), BF16),
            pltpu.VMEM((w_in.shape[0], cells), BF16),
            pltpu.VMEM((hid, cells), F32),
            pltpu.VMEM((3 * hid, cells + 2 * LANES), BF16),
            pltpu.VMEM((3 * hid, cells + LANES), BF16),
            pltpu.VMEM((taps, cells), F32),
            pltpu.VMEM((ch, cells + 2 * LANES), BF16),
        ],
        compiler_params=pltpu.CompilerParams(vmem_limit_bytes=VMEM_LIMIT),
        name="refine",
    )(tiles, w_in, w_qkv, w_proj, w_mid, w_up, w_down, w_out)


def decode_kernel(
    where_ref, pieces_ref, w_in, w_mid, out_ref, t_in, t_mid, strip, act, rows_out,
    *, groups, lanes_in_strip, side,
):
    frames, _, ch3, cols = strip.shape
    frames -= 2
    ch = pieces_ref.shape[1] * 0 + ch3
    frame = pl.program_id(0)
    band = out_ref.shape[2]
    dec = out_ref.shape[1]
    tall = band + 4
    ch = w_in.shape[0] // 27
    columns = lanes_in_strip
    lane = lane_iota(LANES)
    low = lane < side
    col = lane_iota(cols)

    @pl.when(frame == 0)
    def _():
        t_in[...] = w_in[...].astype(F32).T.astype(BF16)
        t_mid[...] = w_mid[...].astype(F32).T.astype(BF16)
        strip[0:2] = jnp.zeros((2,) + strip.shape[1:], BF16)
        note_at = tall * side // LANES * ch
        notes = [
            [pieces_ref[g * columns + d, note_at : note_at + 1, :].astype(F32) for d in range(columns)]
            for g in range(groups)
        ]
        for f in range(frames):
            picks = [
                [jnp.where(notes[g][d] == f, 1.0, 0.0) for d in range(columns)]
                for g in range(groups)
            ]
            for j in range(tall // 2):
                both = []
                for d in range(columns):
                    both.append(
                        sum(
                            pieces_ref[g * columns + d, j * ch : (j + 1) * ch, :].astype(F32)
                            * picks[g][d]
                            for g in range(groups)
                        )
                    )
                turned = [pltpu.roll(x, side, 1) for x in both]
                first = [
                    jnp.where(low, both[d], turned[d + 1]) for d in range(0, columns, 2)
                ]
                second = [
                    jnp.where(low, turned[d], both[d + 1]) for d in range(0, columns, 2)
                ]
                for y, parts in ((2 * j, first), (2 * j + 1, second)):
                    line = jnp.concatenate(parts, axis=1)
                    left = jnp.where(col > 0, pltpu.roll(line, 1, 1), 0.0)
                    right = jnp.where(col < cols - 1, pltpu.roll(line, cols - 1, 1), 0.0)
                    strip[f + 2, y] = jnp.concatenate([left, line, right], axis=0).astype(BF16)

    first_row = where_ref[0] == 0
    last_row = where_ref[0] == where_ref[1] - 1

    def act_row(y, _):
        around = jnp.concatenate(
            [
                strip[pl.ds(frame + dt, 1), pl.ds(y + dy, 1)].reshape(3 * ch, cols)
                for dt in range(3)
                for dy in range(3)
            ],
            axis=0,
        )
        value = silu(dot(t_in[...], around))
        outside = (first_row & (y == 0)) | (last_row & (y == band + 1))
        value = jnp.where(outside, 0.0, value)
        left = jnp.where(col > 0, pltpu.roll(value, 1, 1), 0.0)
        right = jnp.where(col < cols - 1, pltpu.roll(value, cols - 1, 1), 0.0)
        base = pl.multiple_of(y * 3 * dec, 3 * dec)
        act[pl.ds(base, dec), :] = left.astype(BF16)
        act[pl.ds(base + dec, dec), :] = value.astype(BF16)
        act[pl.ds(base + 2 * dec, dec), :] = right.astype(BF16)
        return 0

    lax.fori_loop(0, band + 2, act_row, 0)

    def out_row(y, _):
        base = pl.multiple_of(y * 3 * dec, 3 * dec)
        value = dot(t_mid[...], act[pl.ds(base, 9 * dec), :])
        value = value + act[pl.ds(base + 4 * dec, dec), :].astype(F32)
        for k in range(cols // LANES):
            rows_out[pl.ds(k * dec * band + y, dec, stride=band), :] = value[
                :, k * LANES : (k + 1) * LANES
            ]
        return 0

    lax.fori_loop(0, band, out_row, 0)
    for k in range(cols // LANES):
        done = rows_out[k * dec * band : (k + 1) * dec * band, :]
        out_ref[0, :, :, k * LANES : (k + 1) * LANES] = done.reshape(dec, band, LANES).astype(BF16)


def decode_band(where, pieces, dec_in, dec_mid, frames, groups, columns, side):
    ch, dec = dec_in.shape[3:]
    count, rows, _ = pieces.shape
    band = (rows - META) // ch * LANES // side - 4
    cols = columns * side
    whole = pl.BlockSpec(memory_space=pltpu.VMEM)
    w_in = dec_in.reshape(-1, dec)
    w_mid = dec_mid.reshape(-1, dec)
    return pl.pallas_call(
        functools.partial(decode_kernel, groups=groups, lanes_in_strip=columns, side=side),
        out_shape=jax.ShapeDtypeStruct((frames, dec, band, cols), BF16),
        grid_spec=pltpu.PrefetchScalarGridSpec(
            num_scalar_prefetch=1,
            grid=(frames,),
            in_specs=[whole, whole, whole],
            out_specs=pl.BlockSpec((1, dec, band, cols), lambda f, w: (f, 0, 0, 0)),
            scratch_shapes=[
                pltpu.VMEM((dec, w_in.shape[0]), BF16),
                pltpu.VMEM((dec, w_mid.shape[0]), BF16),
                pltpu.VMEM((frames + 2, band + 4, 3 * ch, cols), BF16),
                pltpu.VMEM(((band + 2) * 3 * dec, cols), BF16),
                pltpu.VMEM((cols // LANES * dec * band, LANES), F32),
            ],
        ),
        compiler_params=pltpu.CompilerParams(vmem_limit_bytes=VMEM_LIMIT),
        name="decode",
    )(where, pieces, w_in, w_mid)


def shards(latent, tile_routes, w_in, w_qkv, w_proj, w_mid, w_up, w_down, w_out, dec_in, dec_mid):
    groups = lax.axis_size("pool")
    columns = lax.axis_size("dev")
    own_tiles = latent[0]
    frames, ch, cells = own_tiles.shape
    side = math.isqrt(cells)
    outgoing = pick_tiles(tile_routes.reshape(-1), own_tiles, groups)
    landing = lax.all_to_all(outgoing, "pool", split_axis=0, concat_axis=0, tiled=True)
    weights = (w_in[0], w_qkv[0], w_proj[0], w_mid[0], w_up[0], w_down[0], w_out[0])
    chunks = refine_tiles(landing, weights, columns)
    pieces = lax.all_to_all(chunks, ("pool", "dev"), split_axis=0, concat_axis=0, tiled=True)
    where = jnp.stack([lax.axis_index("dev"), jnp.int32(columns)])
    return decode_band(where, pieces, dec_in, dec_mid, frames, groups, columns, side)[None]


def solution(mesh):
    in_specs = (
        P("pool", None, None, "dev"),
        P("pool", "dev", None, None),
        P("pool", None, None, None, None),
        P("pool", None, None),
        P("pool", None, None),
        P("pool", None, None, None, None),
        P("pool", None, None),
        P("pool", None, None),
        P("pool", None, None, None, None),
        P(),
        P(),
    )
    out_specs = P("pool", None, None, "dev", None)
    return jax.shard_map(shards, mesh=mesh, in_specs=in_specs, out_specs=out_specs, check_vma=False)
```

```python
import functools
import math

import jax
import jax.numpy as jnp
from jax import lax
from jax.experimental import pallas as pl
from jax.experimental.pallas import tpu as pltpu
from jax.sharding import PartitionSpec as P

HEAD = 64
WIN = 8
LANES = 128
META = 8
EPS = 1e-06
F32 = jnp.float32
BF16 = jnp.bfloat16
VMEM_LIMIT = 60 * 2**20


def dot(a, b):
    return jnp.dot(a, b, preferred_element_type=F32)


def dot_tn(a, b):
    return lax.dot_general(a, b, (((0,), (0,)), ((), ())), preferred_element_type=F32)


def silu(x):
    half = 0.5 * x
    return half + half * jnp.tanh(half)


def norm_channels(x):
    mean = jnp.mean(x * x, axis=0, keepdims=True)
    return x * lax.rsqrt(mean + EPS)


def lane_iota(width):
    return lax.broadcasted_iota(jnp.int32, (1, width), 1)


def pick_kernel(routes_ref, tile_ref, out_ref):
    groups, ch, width = out_ref.shape
    frames, _, cells = tile_ref.shape
    rows = lax.broadcasted_iota(jnp.int32, (ch, LANES), 0)
    for group in range(groups):
        named = functools.reduce(
            jnp.logical_or, [routes_ref[f] == group for f in range(frames)]
        )
        wanted = jnp.where(named, group, groups)
        frame = sum(jnp.where(routes_ref[f] == wanted, f, 0) for f in range(frames))
        out_ref[group, :, :cells] = tile_ref[frame]
        live = jnp.where(named, 1, 0)
        out_ref[group, :, cells:] = jnp.where(rows < META, frame, live).astype(F32).astype(BF16)


def pick_tiles(routes, own_tiles, groups):
    frames, ch, cells = own_tiles.shape
    assert frames == groups
    whole = pl.BlockSpec(memory_space=pltpu.VMEM)
    return pl.pallas_call(
        pick_kernel,
        out_shape=jax.ShapeDtypeStruct((groups, ch, cells + LANES), BF16),
        in_specs=[pl.BlockSpec(memory_space=pltpu.SMEM), whole],
        out_specs=whole,
        name="pick",
    )(routes, own_tiles)


def refine_kernel(*refs, side, bands, first):
    if first:
        _, tile_ref, w_in, w_qkv, w_proj, w_mid, w_up, w_down, w_out = refs[:9]
        out_ref, t_in, t_qkv, t_proj, t_mid, t_up, t_down, perm = refs[9:17]
        scratch = refs[17:]
    else:
        _, tile_ref, _, w_out, t_in, t_qkv, t_proj, t_mid, t_up, t_down, perm = refs[:11]
        out_ref = refs[11]
        scratch = refs[12:]
    patch, att, even, odd, taps, padded, qkv_ref, mixed_ref = scratch
    ch = tile_ref.shape[1]
    cells = side * side
    hid = t_proj.shape[0]
    chunk = WIN * side
    chunks = cells // chunk
    heads = hid // HEAD
    win_cells = WIN * WIN
    pair = LANES // win_cells
    assert side == WIN * WIN and pair == 2 and 2 * side == LANES

    if first:
        for flipped, weight in (
            (t_in, w_in), (t_qkv, w_qkv), (t_proj, w_proj),
            (t_mid, w_mid), (t_up, w_up), (t_down, w_down),
        ):
            flipped[...] = weight[...].astype(F32).T.astype(BF16)
        src = lax.broadcasted_iota(jnp.int32, (chunk, chunk), 0)
        dst = lax.broadcasted_iota(jnp.int32, (chunk, chunk), 1)
        want = ((dst >> 3) & 7) * side + (dst >> 6) * WIN + (dst & 7)
        perm[...] = jnp.where(src == want, 1.0, 0.0).astype(BF16)

    @pl.when(pl.program_id(0) == 0)
    def _():
        even[:, :LANES] = jnp.zeros((3 * hid, LANES), BF16)
        even[:, LANES + cells :] = jnp.zeros((3 * hid, LANES), BF16)
        padded[:, :LANES] = jnp.zeros((ch, LANES), BF16)
        padded[:, LANES + cells :] = jnp.zeros((ch, LANES), BF16)

    tile = tile_ref[0, :, :cells].astype(F32)
    lane = lane_iota(cells)
    row = lane >> 6
    col = lane & (side - 1)

    def inside(dy, dx):
        ok = None
        for pos, off in ((row, dy), (col, dx)):
            if off:
                good = (pos > 0) if off < 0 else (pos < side - 1)
                ok = good if ok is None else ok & good
        return ok

    def moved(x, dy, dx):
        off = dy * side + dx
        if off == 0:
            return x
        x = pltpu.roll(x, (-off) % cells, 1)
        return jnp.where(inside(dy, dx), x, 0.0)

    offsets = [(dy, dx) for dy in (-1, 0, 1) for dx in (-1, 0, 1)]
    for t, (dy, dx) in enumerate(offsets):
        patch[t * ch : (t + 1) * ch, :] = moved(tile, dy, dx).astype(BF16)

    low = lane_iota(LANES) < win_cells
    ccol = lane_iota(chunk) & (side - 1)
    scale = math.log2(math.e) / math.sqrt(HEAD)

    def lift(base):
        lifted = dot(t_in[...], patch[:, pl.ds(base, chunk)])
        att[:, pl.ds(base, chunk)] = lifted
        normed = norm_channels(lifted).astype(BF16)
        windows = dot(normed, perm[...]).astype(BF16)
        qkv_ref[:, pl.ds(base, chunk)] = dot(t_qkv[...], windows).astype(BF16)

    head_of = lax.broadcasted_iota(jnp.int32, (1, hid), 1) < HEAD
    zero = jnp.zeros((HEAD, LANES), BF16)

    def attend(base):
        tiles = [pl.ds(pl.multiple_of(base + p * LANES, LANES), LANES) for p in range(chunk // LANES)]
        scores = []
        for at in tiles:
            keys = qkv_ref[hid : 2 * hid, at].T
            both = jnp.concatenate(
                [jnp.where(head_of, keys, 0), jnp.where(head_of, 0, keys)], axis=0
            ).astype(BF16)
            scores.append(dot(both, qkv_ref[:hid, at]))
        spreads = []
        for full in scores:
            spread = []
            for h in range(heads):
                top = h * LANES
                own = jnp.where(low, full[top : top + win_cells], full[top + win_cells : top + LANES])
                most = jnp.max(own, axis=0, keepdims=True)
                raised = jnp.exp2((own - most) * scale)
                total = jnp.sum(raised, axis=0, keepdims=True)
                probs = raised * (1.0 / total)
                spread += [jnp.where(low, probs, 0.0), jnp.where(low, 0.0, probs)]
            spreads.append(jnp.concatenate(spread, axis=0).astype(BF16))
        for at, spread in zip(tiles, spreads):
            values = jnp.concatenate(
                [
                    jnp.concatenate([qkv_ref[2 * hid : 2 * hid + HEAD, at], zero], axis=1),
                    jnp.concatenate([zero, qkv_ref[2 * hid + HEAD :, at]], axis=1),
                ],
                axis=0,
            )
            mixed_ref[:, at] = dot(values, spread).astype(BF16)

    def project(base):
        mixed = dot(mixed_ref[:, pl.ds(base, chunk)], perm[...]).astype(BF16)
        attended = att[:, pl.ds(base, chunk)] + dot(t_proj[...], mixed)
        att[:, pl.ds(base, chunk)] = attended
        conv_in = norm_channels(attended).astype(BF16)
        left = jnp.where(ccol > 0, pltpu.roll(conv_in, 1, 1), 0)
        right = jnp.where(ccol < side - 1, pltpu.roll(conv_in, chunk - 1, 1), 0)
        here = pl.ds(pl.multiple_of(base + LANES, LANES), chunk)
        even[:hid, here] = left.astype(BF16)
        even[hid : 2 * hid, here] = conv_in
        even[2 * hid :, here] = right.astype(BF16)

    def shift(base):
        around = even[:, pl.ds(base, chunk + LANES)]
        odd[:, pl.ds(base, chunk)] = around[:, side : side + chunk]

    def finish(base):
        after = pl.ds(pl.multiple_of(base + LANES, LANES), chunk)
        around = jnp.concatenate(
            [odd[:, pl.ds(base, chunk)], even[:, after], odd[:, after]], axis=0
        )
        convolved = att[:, pl.ds(base, chunk)] + silu(dot(t_mid[...], around))
        mlp_in = norm_channels(convolved).astype(BF16)
        expanded = silu(dot(t_up[...], mlp_in)).astype(BF16)
        finished = convolved + dot(t_down[...], expanded)
        taps[:, pl.ds(base, chunk)] = dot(w_out[...], finished.astype(BF16))

    for c in range(chunks):
        lift(c * chunk)
    for c in range(chunks):
        attend(c * chunk)
    for c in range(chunks):
        project(c * chunk)
    for c in range(chunks):
        shift(c * chunk)
    odd[:, cells:] = even[:, cells : cells + 2 * LANES][:, side : side + LANES]
    for c in range(chunks):
        finish(c * chunk)

    delta = jnp.zeros((ch, cells), F32)
    for t, (dy, dx) in enumerate(offsets):
        delta = delta + moved(taps[t * ch : (t + 1) * ch, :], dy, dx)
    delta = delta.astype(BF16).astype(F32)
    note = tile_ref[0, :, cells:]
    live = note[META : META + 1, :1].astype(F32)
    padded[:, LANES : LANES + cells] = (tile + live * delta).astype(BF16)
    band = cells // bands
    pieces = (band + 2 * LANES) // LANES
    for b in range(bands):
        for j in range(pieces):
            at = b * band + j * LANES
            out_ref[b, j * ch : (j + 1) * ch, :] = padded[:, at : at + LANES]
        out_ref[b, pieces * ch :, :] = note[:META, :]


def refine_tiles(order, tiles, weights, bands, before=None):
    _, ch, width = tiles.shape
    cells = width - LANES
    side = math.isqrt(cells)
    first = before is None
    if first:
        w_in, w_qkv, w_proj, w_mid, w_up, w_down, w_out = weights
        hid = w_proj.shape[0]
        w_in = w_in.reshape(-1, hid)
        w_mid = w_mid.reshape(-1, hid)
        w_out = jnp.swapaxes(w_out, 2, 3).reshape(-1, hid)
        operands = (w_in, w_qkv, w_proj, w_mid, w_up, w_down, w_out)
        chunk = WIN * side
        flipped = [jax.ShapeDtypeStruct(w.shape[::-1], BF16) for w in operands[:-1]]
        flipped.append(jax.ShapeDtypeStruct((chunk, chunk), BF16))
    else:
        chunks, w_out, *rest = before
        operands = (chunks, w_out, *rest)
        hid = w_out.shape[1]
        flipped = []
    taps = w_out.shape[0]
    rows = (cells // bands + 2 * LANES) // LANES * ch + META
    whole = pl.BlockSpec(memory_space=pltpu.VMEM)
    in_specs = [pl.BlockSpec((1, ch, width), lambda i, o: (o[i], 0, 0))]
    in_specs += [whole if first else pl.BlockSpec(memory_space=pl.ANY)] + [whole] * (len(operands) - 1)
    steps = order.shape[0]
    results = pl.pallas_call(
        functools.partial(refine_kernel, side=side, bands=bands, first=first),
        out_shape=[jax.ShapeDtypeStruct((tiles.shape[0] * bands, rows, LANES), BF16)] + flipped,
        grid_spec=pltpu.PrefetchScalarGridSpec(
            num_scalar_prefetch=1,
            grid=(steps,),
            in_specs=in_specs,
            out_specs=[pl.BlockSpec((bands, rows, LANES), lambda i, o: (o[i], 0, 0))]
            + [whole] * len(flipped),
            scratch_shapes=[
                pltpu.VMEM((taps, cells), BF16),
                pltpu.VMEM((hid, cells), F32),
                pltpu.VMEM((3 * hid, cells + 2 * LANES), BF16),
                pltpu.VMEM((3 * hid, cells + LANES), BF16),
                pltpu.VMEM((taps, cells), F32),
                pltpu.VMEM((ch, cells + 2 * LANES), BF16),
                pltpu.VMEM((3 * hid, cells), BF16),
                pltpu.VMEM((hid, cells), BF16),
            ],
        ),
        input_output_aliases={} if first else {2: 0},
        compiler_params=pltpu.CompilerParams(vmem_limit_bytes=VMEM_LIMIT),
        cost_estimate=pl.CostEstimate(
            flops=steps * 4 * 10**9, bytes_accessed=steps * 2**21, transcendentals=steps * 3 * 10**6
        ),
        name="refine_own" if first else "refine_rest",
    )(order, tiles, *operands)
    return [results[0], w_out, *results[1:]] if first else results[0]


def decode_kernel(
    where_ref, pieces_ref, w_in, w_mid, out_ref, t_in, t_mid, strip, act, rows_out,
    *, groups, lanes_in_strip, side,
):
    frames, _, _, cols = strip.shape
    frames -= 2
    frame = pl.program_id(0)
    band = out_ref.shape[2]
    dec = out_ref.shape[1]
    tall = band + 4
    ch = w_in.shape[0] // 27
    columns = lanes_in_strip
    lane = lane_iota(LANES)
    low = lane < side
    col = lane_iota(cols)

    @pl.when(frame == 0)
    def _():
        t_in[...] = w_in[...].astype(F32).T.astype(BF16)
        t_mid[...] = w_mid[...].astype(F32).T.astype(BF16)
        strip[0:2] = jnp.zeros((2,) + strip.shape[1:], BF16)
        note_at = tall * side // LANES * ch
        notes = [
            [pieces_ref[g * columns + d, note_at : note_at + 1, :].astype(F32) for d in range(columns)]
            for g in range(groups)
        ]
        for f in range(frames):
            picks = [
                [jnp.where(notes[g][d] == f, 1.0, 0.0) for d in range(columns)]
                for g in range(groups)
            ]
            for j in range(tall // 2):
                both = []
                for d in range(columns):
                    both.append(
                        sum(
                            pieces_ref[g * columns + d, j * ch : (j + 1) * ch, :].astype(F32)
                            * picks[g][d]
                            for g in range(groups)
                        )
                    )
                turned = [pltpu.roll(x, side, 1) for x in both]
                first = [
                    jnp.where(low, both[d], turned[d + 1]) for d in range(0, columns, 2)
                ]
                second = [
                    jnp.where(low, turned[d], both[d + 1]) for d in range(0, columns, 2)
                ]
                for y, parts in ((2 * j, first), (2 * j + 1, second)):
                    line = jnp.concatenate(parts, axis=1)
                    left = jnp.where(col > 0, pltpu.roll(line, 1, 1), 0.0)
                    right = jnp.where(col < cols - 1, pltpu.roll(line, cols - 1, 1), 0.0)
                    strip[f + 2, y] = jnp.concatenate([left, line, right], axis=0).astype(BF16)

    first_row = where_ref[0] == 0
    last_row = where_ref[0] == where_ref[1] - 1

    def act_row(y, _):
        around = jnp.concatenate(
            [
                strip[pl.ds(frame + dt, 1), pl.ds(y + dy, 1)].reshape(3 * ch, cols)
                for dt in range(3)
                for dy in range(3)
            ],
            axis=0,
        )
        value = silu(dot(t_in[...], around))
        if y == 0:
            value = jnp.where(first_row, 0.0, value)
        if y == band + 1:
            value = jnp.where(last_row, 0.0, value)
        value = value.astype(BF16)
        left = jnp.where(col > 0, pltpu.roll(value, 1, 1), 0).astype(BF16)
        right = jnp.where(col < cols - 1, pltpu.roll(value, cols - 1, 1), 0).astype(BF16)
        base = y * 3 * dec
        act[pl.ds(base, dec), :] = left
        act[pl.ds(base + dec, dec), :] = value
        act[pl.ds(base + 2 * dec, dec), :] = right
        return 0


    def out_row(y, _):
        base = y * 3 * dec
        value = dot(t_mid[...], act[pl.ds(base, 9 * dec), :])
        value = value + act[pl.ds(base + 4 * dec, dec), :].astype(F32)
        for k in range(cols // LANES):
            rows_out[pl.ds(k * dec * band + y, dec, stride=band), :] = value[
                :, k * LANES : (k + 1) * LANES
            ]
        return 0

    for y in range(band + 2):
        act_row(y, 0)
    for y in range(band):
        out_row(y, 0)
    for k in range(cols // LANES):
        done = rows_out[k * dec * band : (k + 1) * dec * band, :]
        out_ref[0, :, :, k * LANES : (k + 1) * LANES] = done.reshape(dec, band, LANES).astype(BF16)


def decode_band(where, pieces, dec_in, dec_mid, frames, groups, columns, side):
    ch, dec = dec_in.shape[3:]
    count, rows, _ = pieces.shape
    band = (rows - META) // ch * LANES // side - 4
    cols = columns * side
    whole = pl.BlockSpec(memory_space=pltpu.VMEM)
    w_in = dec_in.reshape(-1, dec)
    w_mid = dec_mid.reshape(-1, dec)
    return pl.pallas_call(
        functools.partial(decode_kernel, groups=groups, lanes_in_strip=columns, side=side),
        out_shape=jax.ShapeDtypeStruct((frames, dec, band, cols), BF16),
        grid_spec=pltpu.PrefetchScalarGridSpec(
            num_scalar_prefetch=1,
            grid=(frames,),
            in_specs=[whole, whole, whole],
            out_specs=pl.BlockSpec((1, dec, band, cols), lambda f, w: (f, 0, 0, 0)),
            scratch_shapes=[
                pltpu.VMEM((dec, w_in.shape[0]), BF16),
                pltpu.VMEM((dec, w_mid.shape[0]), BF16),
                pltpu.VMEM((frames + 2, band + 4, 3 * ch, cols), BF16),
                pltpu.VMEM(((band + 2) * 3 * dec, cols), BF16),
                pltpu.VMEM((cols // LANES * dec * band, LANES), F32),
            ],
        ),
        compiler_params=pltpu.CompilerParams(vmem_limit_bytes=VMEM_LIMIT),
        name="decode",
    )(where, pieces, w_in, w_mid)


def shards(latent, tile_routes, w_in, w_qkv, w_proj, w_mid, w_up, w_down, w_out, dec_in, dec_mid):
    groups = lax.axis_size("pool")
    columns = lax.axis_size("dev")
    own_tiles = latent[0]
    frames, ch, cells = own_tiles.shape
    side = math.isqrt(cells)
    outgoing = pick_tiles(tile_routes.reshape(-1), own_tiles, groups)
    landing = lax.all_to_all(outgoing, "pool", split_axis=0, concat_axis=0, tiled=True)
    weights = (w_in[0], w_qkv[0], w_proj[0], w_mid[0], w_up[0], w_down[0], w_out[0])
    order = (lax.axis_index("pool") + jnp.arange(groups, dtype=jnp.int32)) % groups
    done = refine_tiles(order[:1], outgoing, weights, columns)
    chunks = refine_tiles(order[1:], landing, None, columns, done)
    pieces = lax.all_to_all(chunks, ("pool", "dev"), split_axis=0, concat_axis=0, tiled=True)
    where = jnp.stack([lax.axis_index("dev"), jnp.int32(columns)])
    return decode_band(where, pieces, dec_in, dec_mid, frames, groups, columns, side)[None]


def solution(mesh):
    in_specs = (
        P("pool", None, None, "dev"),
        P("pool", "dev", None, None),
        P("pool", None, None, None, None),
        P("pool", None, None),
        P("pool", None, None),
        P("pool", None, None, None, None),
        P("pool", None, None),
        P("pool", None, None),
        P("pool", None, None, None, None),
        P(),
        P(),
    )
    out_specs = P("pool", None, None, "dev", None)
    return jax.shard_map(shards, mesh=mesh, in_specs=in_specs, out_specs=out_specs, check_vma=False)
```

```python
import functools
import math

import jax
import jax.numpy as jnp
from jax import lax
from jax.experimental import pallas as pl
from jax.experimental.pallas import tpu as pltpu
from jax.sharding import PartitionSpec as P

HEAD = 64
WIN = 8
LANES = 128
META = 8
EPS = 1e-06
F32 = jnp.float32
BF16 = jnp.bfloat16
VMEM_LIMIT = 60 * 2**20


def dot(a, b):
    return jnp.dot(a, b, preferred_element_type=F32)


def dot_tn(a, b):
    return lax.dot_general(a, b, (((0,), (0,)), ((), ())), preferred_element_type=F32)


def silu(x):
    half = 0.5 * x
    return half + half * jnp.tanh(half)


def norm_channels(x):
    mean = jnp.mean(x * x, axis=0, keepdims=True)
    return x * lax.rsqrt(mean + EPS)


def lane_iota(width):
    return lax.broadcasted_iota(jnp.int32, (1, width), 1)


def pick_kernel(routes_ref, tile_ref, out_ref):
    groups, ch, width = out_ref.shape
    frames, _, cells = tile_ref.shape
    rows = lax.broadcasted_iota(jnp.int32, (ch, LANES), 0)
    for group in range(groups):
        named = functools.reduce(
            jnp.logical_or, [routes_ref[f] == group for f in range(frames)]
        )
        wanted = jnp.where(named, group, groups)
        frame = sum(jnp.where(routes_ref[f] == wanted, f, 0) for f in range(frames))
        out_ref[group, :, :cells] = tile_ref[frame]
        live = jnp.where(named, 1, 0)
        out_ref[group, :, cells:] = jnp.where(rows < META, frame, live).astype(F32).astype(BF16)


def pick_tiles(routes, own_tiles, groups):
    frames, ch, cells = own_tiles.shape
    assert frames == groups
    whole = pl.BlockSpec(memory_space=pltpu.VMEM)
    return pl.pallas_call(
        pick_kernel,
        out_shape=jax.ShapeDtypeStruct((groups, ch, cells + LANES), BF16),
        in_specs=[pl.BlockSpec(memory_space=pltpu.SMEM), whole],
        out_specs=whole,
        name="pick",
    )(routes, own_tiles)


def refine_kernel(*refs, side, bands, first):
    if first:
        _, tile_ref, w_in, w_qkv, w_proj, w_mid, w_up, w_down, w_out = refs[:9]
        out_ref, t_in, t_qkv, t_proj, t_mid, t_up, t_down, perm = refs[9:17]
        scratch = refs[17:]
    else:
        _, tile_ref, _, w_out, t_in, t_qkv, t_proj, t_mid, t_up, t_down, perm = refs[:11]
        out_ref = refs[11]
        scratch = refs[12:]
    patch, att, even, odd, taps, padded, qkv_ref, mixed_ref, wide, wide_f = scratch
    ch = tile_ref.shape[1]
    cells = side * side
    hid = t_proj.shape[0]
    chunk = WIN * side
    chunks = cells // chunk
    heads = hid // HEAD
    win_cells = WIN * WIN
    pair = LANES // win_cells
    assert side == WIN * WIN and pair == 2 and 2 * side == LANES

    if first:
        for flipped, weight in (
            (t_in, w_in), (t_qkv, w_qkv), (t_proj, w_proj),
            (t_mid, w_mid), (t_up, w_up), (t_down, w_down),
        ):
            flipped[...] = weight[...].astype(F32).T.astype(BF16)
        src = lax.broadcasted_iota(jnp.int32, (chunk, chunk), 0)
        dst = lax.broadcasted_iota(jnp.int32, (chunk, chunk), 1)
        want = ((dst >> 3) & 7) * side + (dst >> 6) * WIN + (dst & 7)
        perm[...] = jnp.where(src == want, 1.0, 0.0).astype(BF16)

    @pl.when(pl.program_id(0) == 0)
    def _():
        even[:, :LANES] = jnp.zeros((3 * hid, LANES), BF16)
        even[:, LANES + cells :] = jnp.zeros((3 * hid, LANES), BF16)
        padded[:, :LANES] = jnp.zeros((ch, LANES), BF16)
        padded[:, LANES + cells :] = jnp.zeros((ch, LANES), BF16)

    tile = tile_ref[0, :, :cells].astype(F32)
    lane = lane_iota(cells)
    row = lane >> 6
    col = lane & (side - 1)

    def inside(dy, dx):
        ok = None
        for pos, off in ((row, dy), (col, dx)):
            if off:
                good = (pos > 0) if off < 0 else (pos < side - 1)
                ok = good if ok is None else ok & good
        return ok

    def moved(x, dy, dx):
        off = dy * side + dx
        if off == 0:
            return x
        x = pltpu.roll(x, (-off) % cells, 1)
        return jnp.where(inside(dy, dx), x, 0.0)

    offsets = [(dy, dx) for dy in (-1, 0, 1) for dx in (-1, 0, 1)]
    for t, (dy, dx) in enumerate(offsets):
        patch[t * ch : (t + 1) * ch, :] = moved(tile, dy, dx).astype(BF16)

    low = lane_iota(LANES) < win_cells
    ccol = lane_iota(chunk) & (side - 1)
    scale = math.log2(math.e) / math.sqrt(HEAD)

    def lift(base):
        lifted = dot(t_in[...], patch[:, pl.ds(base, chunk)])
        att[:, pl.ds(base, chunk)] = lifted
        mixed_ref[:, pl.ds(base, chunk)] = norm_channels(lifted).astype(BF16)

    def lift2(base):
        mixed_ref[:, pl.ds(base, chunk)] = dot(mixed_ref[:, pl.ds(base, chunk)], perm[...]).astype(BF16)

    def lift3(base):
        qkv_ref[:, pl.ds(base, chunk)] = dot(t_qkv[...], mixed_ref[:, pl.ds(base, chunk)]).astype(BF16)

    head_of = lax.broadcasted_iota(jnp.int32, (1, hid), 1) < HEAD
    zero = jnp.zeros((HEAD, LANES), BF16)

    def attend(base):
        for p in range(chunk // LANES):
            at = pl.ds(base + p * LANES, LANES)
            keys = qkv_ref[hid : 2 * hid, at].T
            both = jnp.concatenate(
                [jnp.where(head_of, keys, 0), jnp.where(head_of, 0, keys)], axis=0
            ).astype(BF16)
            full = dot(both, qkv_ref[:hid, at])
            for h in range(heads):
                top = h * LANES
                wide_f[h * win_cells : (h + 1) * win_cells, at] = jnp.where(
                    low, full[top : top + win_cells], full[top + win_cells : top + LANES]
                )

    def attend2(base):
        for p in range(chunk // LANES):
            at = pl.ds(base + p * LANES, LANES)
            for h in range(heads):
                own = wide_f[h * win_cells : (h + 1) * win_cells, at]
                most = jnp.max(own, axis=0, keepdims=True)
                raised = jnp.exp2((own - most) * scale)
                total = jnp.sum(raised, axis=0, keepdims=True)
                probs = (raised * (1.0 / total)).astype(BF16)
                top = h * LANES
                wide[top : top + win_cells, at] = jnp.where(low, probs, 0)
                wide[top + win_cells : top + LANES, at] = jnp.where(low, 0, probs)

    def attend3(base):
        for p in range(chunk // LANES):
            at = pl.ds(base + p * LANES, LANES)
            values = jnp.concatenate(
                [
                    jnp.concatenate([qkv_ref[2 * hid : 2 * hid + HEAD, at], zero], axis=1),
                    jnp.concatenate([zero, qkv_ref[2 * hid + HEAD :, at]], axis=1),
                ],
                axis=0,
            )
            mixed_ref[:, at] = dot(values, wide[: heads * LANES, at]).astype(BF16)

    def project(base):
        mixed_ref[:, pl.ds(base, chunk)] = dot(mixed_ref[:, pl.ds(base, chunk)], perm[...]).astype(BF16)

    def project2(base):
        attended = att[:, pl.ds(base, chunk)] + dot(t_proj[...], mixed_ref[:, pl.ds(base, chunk)])
        att[:, pl.ds(base, chunk)] = attended
        here = pl.ds(base + LANES, chunk)
        even[hid : 2 * hid, here] = norm_channels(attended).astype(BF16)

    def project3(base):
        here = pl.ds(base + LANES, chunk)
        conv_in = even[hid : 2 * hid, here]
        even[:hid, here] = jnp.where(ccol > 0, pltpu.roll(conv_in, 1, 1), 0)
        even[2 * hid :, here] = jnp.where(ccol < side - 1, pltpu.roll(conv_in, chunk - 1, 1), 0)

    def shift(base):
        around = even[:, pl.ds(base, chunk + LANES)]
        odd[:, pl.ds(base, chunk)] = around[:, side : side + chunk]

    def finish1(base):
        after = pl.ds(base + LANES, chunk)
        around = jnp.concatenate(
            [odd[:, pl.ds(base, chunk)], even[:, after], odd[:, after]], axis=0
        )
        convolved = att[:, pl.ds(base, chunk)] + silu(dot(t_mid[...], around))
        att[:, pl.ds(base, chunk)] = convolved
        mixed_ref[:, pl.ds(base, chunk)] = norm_channels(convolved).astype(BF16)

    def finish2(base):
        wide[:, pl.ds(base, chunk)] = silu(dot(t_up[...], mixed_ref[:, pl.ds(base, chunk)])).astype(BF16)

    def finish3(base):
        finished = att[:, pl.ds(base, chunk)] + dot(t_down[...], wide[:, pl.ds(base, chunk)])
        mixed_ref[:, pl.ds(base, chunk)] = finished.astype(BF16)

    def finish4(base):
        taps[:, pl.ds(base, chunk)] = dot(w_out[...], mixed_ref[:, pl.ds(base, chunk)])

    lags = (
        (finish4, 14), (finish3, 13), (finish2, 12), (finish1, 11), (shift, 9), (project3, 8),
        (project2, 7), (project, 6), (attend3, 5), (attend2, 4), (attend, 3), (lift3, 2), (lift2, 1), (lift, 0),
    )
    for step in range(chunks + 14):
        for body, lag in lags:
            if 0 <= step - lag < chunks:
                body((step - lag) * chunk)
                if body is shift and step - lag == chunks - 1:
                    odd[:, cells:] = even[:, cells : cells + 2 * LANES][:, side : side + LANES]

    delta = jnp.zeros((ch, cells), F32)
    for t, (dy, dx) in enumerate(offsets):
        delta = delta + moved(taps[t * ch : (t + 1) * ch, :], dy, dx)
    delta = delta.astype(BF16).astype(F32)
    note = tile_ref[0, :, cells:]
    live = note[META : META + 1, :1].astype(F32)
    padded[:, LANES : LANES + cells] = (tile + live * delta).astype(BF16)
    band = cells // bands
    pieces = (band + 2 * LANES) // LANES
    for b in range(bands):
        for j in range(pieces):
            at = b * band + j * LANES
            out_ref[b, j * ch : (j + 1) * ch, :] = padded[:, at : at + LANES]
        out_ref[b, pieces * ch :, :] = note[:META, :]


def refine_tiles(order, tiles, weights, bands, before=None):
    _, ch, width = tiles.shape
    cells = width - LANES
    side = math.isqrt(cells)
    first = before is None
    if first:
        w_in, w_qkv, w_proj, w_mid, w_up, w_down, w_out = weights
        hid = w_proj.shape[0]
        w_in = w_in.reshape(-1, hid)
        w_mid = w_mid.reshape(-1, hid)
        w_out = jnp.swapaxes(w_out, 2, 3).reshape(-1, hid)
        operands = (w_in, w_qkv, w_proj, w_mid, w_up, w_down, w_out)
        chunk = WIN * side
        flipped = [jax.ShapeDtypeStruct(w.shape[::-1], BF16) for w in operands[:-1]]
        flipped.append(jax.ShapeDtypeStruct((chunk, chunk), BF16))
        mlp = w_up.shape[1]
    else:
        chunks, w_out, *rest = before
        operands = (chunks, w_out, *rest)
        hid = w_out.shape[1]
        mlp = rest[4].shape[0]
        flipped = []
    taps = w_out.shape[0]
    rows = (cells // bands + 2 * LANES) // LANES * ch + META
    whole = pl.BlockSpec(memory_space=pltpu.VMEM)
    in_specs = [pl.BlockSpec((1, ch, width), lambda i, o: (o[i], 0, 0))]
    in_specs += [whole if first else pl.BlockSpec(memory_space=pl.ANY)] + [whole] * (len(operands) - 1)
    steps = order.shape[0]
    results = pl.pallas_call(
        functools.partial(refine_kernel, side=side, bands=bands, first=first),
        out_shape=[jax.ShapeDtypeStruct((tiles.shape[0] * bands, rows, LANES), BF16)] + flipped,
        grid_spec=pltpu.PrefetchScalarGridSpec(
            num_scalar_prefetch=1,
            grid=(steps,),
            in_specs=in_specs,
            out_specs=[pl.BlockSpec((bands, rows, LANES), lambda i, o: (o[i], 0, 0))]
            + [whole] * len(flipped),
            scratch_shapes=[
                pltpu.VMEM((taps, cells), BF16),
                pltpu.VMEM((hid, cells), F32),
                pltpu.VMEM((3 * hid, cells + 2 * LANES), BF16),
                pltpu.VMEM((3 * hid, cells + LANES), BF16),
                pltpu.VMEM((taps, cells), F32),
                pltpu.VMEM((ch, cells + 2 * LANES), BF16),
                pltpu.VMEM((3 * hid, cells), BF16),
                pltpu.VMEM((hid, cells), BF16),
                pltpu.VMEM((mlp, cells), BF16),
                pltpu.VMEM((hid, cells), F32),
            ],
        ),
        input_output_aliases={} if first else {2: 0},
        compiler_params=pltpu.CompilerParams(vmem_limit_bytes=VMEM_LIMIT),
        cost_estimate=pl.CostEstimate(
            flops=steps * 4 * 10**9, bytes_accessed=steps * 2**21, transcendentals=steps * 3 * 10**6
        ),
        name="refine_own" if first else "refine_rest",
    )(order, tiles, *operands)
    return [results[0], w_out, *results[1:]] if first else results[0]


def decode_kernel(
    where_ref, pieces_ref, t_in, t_mid, out_ref, strip, act, rows_out,
    *, groups, lanes_in_strip, side,
):
    frames, _, _, cols = strip.shape
    frames -= 2
    frame = pl.program_id(0)
    band = out_ref.shape[2]
    dec = out_ref.shape[1]
    tall = band + 4
    ch = t_in.shape[1] // 27
    columns = lanes_in_strip
    lane = lane_iota(LANES)
    low = lane < side
    col = lane_iota(cols)

    @pl.when(frame == 0)
    def _():
        strip[0:2] = jnp.zeros((2,) + strip.shape[1:], BF16)
        note_at = tall * side // LANES * ch
        notes = [
            [pieces_ref[g * columns + d, note_at : note_at + 1, :].astype(F32) for d in range(columns)]
            for g in range(groups)
        ]
        for f in range(frames):
            picks = [
                [jnp.where(notes[g][d] == f, 1.0, 0.0) for d in range(columns)]
                for g in range(groups)
            ]
            for j in range(tall // 2):
                both = []
                for d in range(columns):
                    both.append(
                        sum(
                            pieces_ref[g * columns + d, j * ch : (j + 1) * ch, :].astype(F32)
                            * picks[g][d]
                            for g in range(groups)
                        )
                    )
                turned = [pltpu.roll(x, side, 1) for x in both]
                first = [
                    jnp.where(low, both[d], turned[d + 1]) for d in range(0, columns, 2)
                ]
                second = [
                    jnp.where(low, turned[d], both[d + 1]) for d in range(0, columns, 2)
                ]
                for y, parts in ((2 * j, first), (2 * j + 1, second)):
                    line = jnp.concatenate(parts, axis=1)
                    left = jnp.where(col > 0, pltpu.roll(line, 1, 1), 0.0)
                    right = jnp.where(col < cols - 1, pltpu.roll(line, cols - 1, 1), 0.0)
                    strip[f + 2, y] = jnp.concatenate([left, line, right], axis=0).astype(BF16)

    first_row = where_ref[0] == 0
    last_row = where_ref[0] == where_ref[1] - 1

    def act_row(y):
        around = jnp.concatenate(
            [
                strip[pl.ds(frame + dt, 1), pl.ds(y + dy, 1)].reshape(3 * ch, cols)
                for dt in range(3)
                for dy in range(3)
            ],
            axis=0,
        )
        value = silu(dot(t_in[...], around))
        if y == 0:
            value = jnp.where(first_row, 0.0, value)
        if y == band + 1:
            value = jnp.where(last_row, 0.0, value)
        top = y * 3 * dec
        act[top + dec : top + 2 * dec, :] = value.astype(BF16)

    def side_rows(y):
        top = y * 3 * dec
        value = act[top + dec : top + 2 * dec, :]
        act[top : top + dec, :] = jnp.where(col > 0, pltpu.roll(value, 1, 1), 0)
        act[top + 2 * dec : top + 3 * dec, :] = jnp.where(
            col < cols - 1, pltpu.roll(value, cols - 1, 1), 0
        )

    def out_row(y):
        top = y * 3 * dec
        value = dot(t_mid[...], act[top : top + 9 * dec, :])
        value = value + act[top + 4 * dec : top + 5 * dec, :].astype(F32)
        for k in range(cols // LANES):
            rows_out[pl.ds(k * dec * band + y, dec, stride=band), :] = value[
                :, k * LANES : (k + 1) * LANES
            ]

    for y in range(band + 2):
        act_row(y)
    for y in range(band + 2):
        side_rows(y)
    for y in range(band):
        out_row(y)
    for k in range(cols // LANES):
        done = rows_out[k * dec * band : (k + 1) * dec * band, :]
        out_ref[0, :, :, k * LANES : (k + 1) * LANES] = done.reshape(dec, band, LANES).astype(BF16)


def flip_kernel(w_in, w_mid, t_in, t_mid):
    t_in[...] = w_in[...].astype(F32).T.astype(BF16)
    t_mid[...] = w_mid[...].astype(F32).T.astype(BF16)


def flip_weights(dec_in, dec_mid):
    dec = dec_in.shape[-1]
    both = (dec_in.reshape(-1, dec), dec_mid.reshape(-1, dec))
    return pl.pallas_call(
        flip_kernel,
        out_shape=[jax.ShapeDtypeStruct(w.shape[::-1], BF16) for w in both],
        in_specs=[pl.BlockSpec(memory_space=pltpu.VMEM)] * 2,
        out_specs=[pl.BlockSpec(memory_space=pltpu.VMEM)] * 2,
        cost_estimate=pl.CostEstimate(flops=10**6, bytes_accessed=2**21, transcendentals=0),
        name="flip",
    )(*both)


def decode_band(where, pieces, t_in, t_mid, frames, groups, columns, side):
    dec = t_in.shape[0]
    ch = t_in.shape[1] // 27
    count, rows, _ = pieces.shape
    band = (rows - META) // ch * LANES // side - 4
    cols = columns * side
    whole = pl.BlockSpec(memory_space=pltpu.VMEM)
    return pl.pallas_call(
        functools.partial(decode_kernel, groups=groups, lanes_in_strip=columns, side=side),
        out_shape=jax.ShapeDtypeStruct((frames, dec, band, cols), BF16),
        grid_spec=pltpu.PrefetchScalarGridSpec(
            num_scalar_prefetch=1,
            grid=(frames,),
            in_specs=[whole, whole, whole],
            out_specs=pl.BlockSpec((1, dec, band, cols), lambda f, w: (f, 0, 0, 0)),
            scratch_shapes=[
                pltpu.VMEM((frames + 2, band + 4, 3 * ch, cols), BF16),
                pltpu.VMEM(((band + 2) * 3 * dec, cols), BF16),
                pltpu.VMEM((cols // LANES * dec * band, LANES), F32),
            ],
        ),
        compiler_params=pltpu.CompilerParams(vmem_limit_bytes=VMEM_LIMIT),
        name="decode",
    )(where, pieces, t_in, t_mid)


def shards(latent, tile_routes, w_in, w_qkv, w_proj, w_mid, w_up, w_down, w_out, dec_in, dec_mid):
    groups = lax.axis_size("pool")
    columns = lax.axis_size("dev")
    own_tiles = latent[0]
    frames, ch, cells = own_tiles.shape
    side = math.isqrt(cells)
    outgoing = pick_tiles(tile_routes.reshape(-1), own_tiles, groups)
    landing = lax.all_to_all(outgoing, "pool", split_axis=0, concat_axis=0, tiled=True)
    weights = (w_in[0], w_qkv[0], w_proj[0], w_mid[0], w_up[0], w_down[0], w_out[0])
    order = (lax.axis_index("pool") + jnp.arange(groups, dtype=jnp.int32)) % groups
    done = refine_tiles(order[:1], outgoing, weights, columns)
    chunks = refine_tiles(order[1:], landing, None, columns, done)
    pieces = lax.all_to_all(chunks, ("pool", "dev"), split_axis=0, concat_axis=0, tiled=True)
    where = jnp.stack([lax.axis_index("dev"), jnp.int32(columns)])
    return decode_band(
        where, pieces, *flip_weights(dec_in, dec_mid), frames, groups, columns, side
    )[None]


def solution(mesh):
    in_specs = (
        P("pool", None, None, "dev"),
        P("pool", "dev", None, None),
        P("pool", None, None, None, None),
        P("pool", None, None),
        P("pool", None, None),
        P("pool", None, None, None, None),
        P("pool", None, None),
        P("pool", None, None),
        P("pool", None, None, None, None),
        P(),
        P(),
    )
    out_specs = P("pool", None, None, "dev", None)
    return jax.shard_map(shards, mesh=mesh, in_specs=in_specs, out_specs=out_specs, check_vma=False)
```

```python
import functools
import math

import jax
import jax.numpy as jnp
from jax import lax
from jax.experimental import pallas as pl
from jax.experimental.pallas import tpu as pltpu
from jax.sharding import PartitionSpec as P

HEAD = 64
WIN = 8
LANES = 128
META = 8
POOL = ("far", "near")
EPS = 1e-06
F32 = jnp.float32
BF16 = jnp.bfloat16
VMEM_LIMIT = 60 * 2**20


def dot(a, b):
    return jnp.dot(a, b, preferred_element_type=F32)


def dot_tn(a, b):
    return lax.dot_general(a, b, (((0,), (0,)), ((), ())), preferred_element_type=F32)


def silu(x):
    half = 0.5 * x
    return half + half * jnp.tanh(half)


def norm_channels(x):
    mean = jnp.mean(x * x, axis=0, keepdims=True)
    return x * lax.rsqrt(mean + EPS)


def lane_iota(width):
    return lax.broadcasted_iota(jnp.int32, (1, width), 1)


def pick_kernel(routes_ref, tile_ref, out_ref):
    groups, ch, width = out_ref.shape
    frames, _, cells = tile_ref.shape
    rows = lax.broadcasted_iota(jnp.int32, (ch, LANES), 0)
    for group in range(groups):
        named = functools.reduce(
            jnp.logical_or, [routes_ref[f] == group for f in range(frames)]
        )
        wanted = jnp.where(named, group, groups)
        frame = sum(jnp.where(routes_ref[f] == wanted, f, 0) for f in range(frames))
        out_ref[group, :, :cells] = tile_ref[frame]
        live = jnp.where(named, 1, 0)
        out_ref[group, :, cells:] = jnp.where(rows < META, frame, live).astype(F32).astype(BF16)


def pick_tiles(routes, own_tiles, groups):
    frames, ch, cells = own_tiles.shape
    assert frames == groups
    whole = pl.BlockSpec(memory_space=pltpu.VMEM)
    return pl.pallas_call(
        pick_kernel,
        out_shape=jax.ShapeDtypeStruct((groups, ch, cells + LANES), BF16),
        in_specs=[pl.BlockSpec(memory_space=pltpu.SMEM), whole],
        out_specs=whole,
        name="pick",
    )(routes, own_tiles)


def refine_kernel(*refs, side, bands, first):
    if first:
        _, tile_ref, w_in, w_qkv, w_proj, w_mid, w_up, w_down, w_out = refs[:9]
        out_ref, t_in, t_qkv, t_proj, t_mid, t_up, t_down, perm = refs[9:17]
        scratch = refs[17:]
    else:
        _, tile_ref, _, w_out, t_in, t_qkv, t_proj, t_mid, t_up, t_down, perm = refs[:11]
        out_ref = refs[11]
        scratch = refs[12:]
    patch, att, even, odd, taps, padded, qkv_ref, mixed_ref, wide, wide_f = scratch
    ch = tile_ref.shape[1]
    cells = side * side
    hid = t_proj.shape[0]
    chunk = WIN * side
    chunks = cells // chunk
    heads = hid // HEAD
    win_cells = WIN * WIN
    pair = LANES // win_cells
    assert side == WIN * WIN and pair == 2 and 2 * side == LANES

    if first:
        for flipped, weight in (
            (t_in, w_in), (t_qkv, w_qkv), (t_proj, w_proj),
            (t_mid, w_mid), (t_up, w_up), (t_down, w_down),
        ):
            flipped[...] = weight[...].astype(F32).T.astype(BF16)
        src = lax.broadcasted_iota(jnp.int32, (chunk, chunk), 0)
        dst = lax.broadcasted_iota(jnp.int32, (chunk, chunk), 1)
        want = ((dst >> 3) & 7) * side + (dst >> 6) * WIN + (dst & 7)
        perm[...] = jnp.where(src == want, 1.0, 0.0).astype(BF16)

    @pl.when(pl.program_id(0) == 0)
    def _():
        even[:, :LANES] = jnp.zeros((3 * hid, LANES), BF16)
        even[:, LANES + cells :] = jnp.zeros((3 * hid, LANES), BF16)
        padded[:, :LANES] = jnp.zeros((ch, LANES), BF16)
        padded[:, LANES + cells :] = jnp.zeros((ch, LANES), BF16)

    tile = tile_ref[0, :, :cells].astype(F32)
    lane = lane_iota(cells)
    row = lane >> 6
    col = lane & (side - 1)

    def inside(dy, dx):
        ok = None
        for pos, off in ((row, dy), (col, dx)):
            if off:
                good = (pos > 0) if off < 0 else (pos < side - 1)
                ok = good if ok is None else ok & good
        return ok

    def moved(x, dy, dx):
        off = dy * side + dx
        if off == 0:
            return x
        x = pltpu.roll(x, (-off) % cells, 1)
        return jnp.where(inside(dy, dx), x, 0.0)

    offsets = [(dy, dx) for dy in (-1, 0, 1) for dx in (-1, 0, 1)]
    for t, (dy, dx) in enumerate(offsets):
        patch[t * ch : (t + 1) * ch, :] = moved(tile, dy, dx).astype(BF16)

    low = lane_iota(LANES) < win_cells
    ccol = lane_iota(chunk) & (side - 1)
    scale = math.log2(math.e) / math.sqrt(HEAD)

    def lift(base):
        lifted = dot(t_in[...], patch[:, pl.ds(base, chunk)])
        att[:, pl.ds(base, chunk)] = lifted
        mixed_ref[:, pl.ds(base, chunk)] = norm_channels(lifted).astype(BF16)

    def lift2(base):
        mixed_ref[:, pl.ds(base, chunk)] = dot(mixed_ref[:, pl.ds(base, chunk)], perm[...]).astype(BF16)

    def lift3(base):
        qkv_ref[:, pl.ds(base, chunk)] = dot(t_qkv[...], mixed_ref[:, pl.ds(base, chunk)]).astype(BF16)

    head_of = lax.broadcasted_iota(jnp.int32, (1, hid), 1) < HEAD
    zero = jnp.zeros((HEAD, LANES), BF16)

    def attend(base):
        for p in range(chunk // LANES):
            at = pl.ds(base + p * LANES, LANES)
            keys = qkv_ref[hid : 2 * hid, at].T
            both = jnp.concatenate(
                [jnp.where(head_of, keys, 0), jnp.where(head_of, 0, keys)], axis=0
            ).astype(BF16)
            full = dot(both, qkv_ref[:hid, at])
            for h in range(heads):
                top = h * LANES
                wide_f[h * win_cells : (h + 1) * win_cells, at] = jnp.where(
                    low, full[top : top + win_cells], full[top + win_cells : top + LANES]
                )

    def attend2(base):
        for p in range(chunk // LANES):
            at = pl.ds(base + p * LANES, LANES)
            for h in range(heads):
                own = wide_f[h * win_cells : (h + 1) * win_cells, at]
                most = jnp.max(own, axis=0, keepdims=True)
                raised = jnp.exp2((own - most) * scale)
                total = jnp.sum(raised, axis=0, keepdims=True)
                probs = (raised * (1.0 / total)).astype(BF16)
                top = h * LANES
                wide[top : top + win_cells, at] = jnp.where(low, probs, 0)
                wide[top + win_cells : top + LANES, at] = jnp.where(low, 0, probs)

    def attend3(base):
        for p in range(chunk // LANES):
            at = pl.ds(base + p * LANES, LANES)
            values = jnp.concatenate(
                [
                    jnp.concatenate([qkv_ref[2 * hid : 2 * hid + HEAD, at], zero], axis=1),
                    jnp.concatenate([zero, qkv_ref[2 * hid + HEAD :, at]], axis=1),
                ],
                axis=0,
            )
            mixed_ref[:, at] = dot(values, wide[: heads * LANES, at]).astype(BF16)

    def project(base):
        mixed_ref[:, pl.ds(base, chunk)] = dot(mixed_ref[:, pl.ds(base, chunk)], perm[...]).astype(BF16)

    def project2(base):
        attended = att[:, pl.ds(base, chunk)] + dot(t_proj[...], mixed_ref[:, pl.ds(base, chunk)])
        att[:, pl.ds(base, chunk)] = attended
        here = pl.ds(base + LANES, chunk)
        even[hid : 2 * hid, here] = norm_channels(attended).astype(BF16)

    def project3(base):
        here = pl.ds(base + LANES, chunk)
        conv_in = even[hid : 2 * hid, here]
        even[:hid, here] = jnp.where(ccol > 0, pltpu.roll(conv_in, 1, 1), 0)
        even[2 * hid :, here] = jnp.where(ccol < side - 1, pltpu.roll(conv_in, chunk - 1, 1), 0)

    def shift(base):
        around = even[:, pl.ds(base, chunk + LANES)]
        odd[:, pl.ds(base, chunk)] = around[:, side : side + chunk]

    def finish1(base):
        after = pl.ds(base + LANES, chunk)
        around = jnp.concatenate(
            [odd[:, pl.ds(base, chunk)], even[:, after], odd[:, after]], axis=0
        )
        convolved = att[:, pl.ds(base, chunk)] + silu(dot(t_mid[...], around))
        att[:, pl.ds(base, chunk)] = convolved
        mixed_ref[:, pl.ds(base, chunk)] = norm_channels(convolved).astype(BF16)

    def finish2(base):
        wide[:, pl.ds(base, chunk)] = silu(dot(t_up[...], mixed_ref[:, pl.ds(base, chunk)])).astype(BF16)

    def finish3(base):
        finished = att[:, pl.ds(base, chunk)] + dot(t_down[...], wide[:, pl.ds(base, chunk)])
        mixed_ref[:, pl.ds(base, chunk)] = finished.astype(BF16)

    def finish4(base):
        taps[:, pl.ds(base, chunk)] = dot(w_out[...], mixed_ref[:, pl.ds(base, chunk)])

    lags = (
        (finish4, 14), (finish3, 13), (finish2, 12), (finish1, 11), (shift, 9), (project3, 8),
        (project2, 7), (project, 6), (attend3, 5), (attend2, 4), (attend, 3), (lift3, 2), (lift2, 1), (lift, 0),
    )
    for step in range(chunks + 14):
        for body, lag in lags:
            if 0 <= step - lag < chunks:
                body((step - lag) * chunk)
                if body is shift and step - lag == chunks - 1:
                    odd[:, cells:] = even[:, cells : cells + 2 * LANES][:, side : side + LANES]

    delta = jnp.zeros((ch, cells), F32)
    for t, (dy, dx) in enumerate(offsets):
        delta = delta + moved(taps[t * ch : (t + 1) * ch, :], dy, dx)
    delta = delta.astype(BF16).astype(F32)
    note = tile_ref[0, :, cells:]
    live = note[META : META + 1, :1].astype(F32)
    padded[:, LANES : LANES + cells] = (tile + live * delta).astype(BF16)
    band = cells // bands
    pieces = (band + 2 * LANES) // LANES
    for b in range(bands):
        for j in range(pieces):
            at = b * band + j * LANES
            out_ref[b, j * ch : (j + 1) * ch, :] = padded[:, at : at + LANES]
        out_ref[b, pieces * ch :, :] = note[:META, :]


def refine_tiles(name, place, tiles, steps, tile_at, slot_at, weights, bands, before=None):
    _, ch, width = tiles.shape
    cells = width - LANES
    side = math.isqrt(cells)
    first = before is None
    keep = False
    if first:
        w_in, w_qkv, w_proj, w_mid, w_up, w_down, w_out = weights
        hid = w_proj.shape[0]
        w_in = w_in.reshape(-1, hid)
        w_mid = w_mid.reshape(-1, hid)
        w_out = jnp.swapaxes(w_out, 2, 3).reshape(-1, hid)
        operands = (w_in, w_qkv, w_proj, w_mid, w_up, w_down, w_out)
        chunk = WIN * side
        flipped = [jax.ShapeDtypeStruct(w.shape[::-1], BF16) for w in operands[:-1]]
        flipped.append(jax.ShapeDtypeStruct((chunk, chunk), BF16))
        mlp = w_up.shape[1]
    else:
        chunks, keep, (w_out, *rest) = before
        operands = (chunks, w_out, *rest)
        hid = w_out.shape[1]
        mlp = rest[4].shape[0]
        flipped = []
    taps = w_out.shape[0]
    rows = (cells // bands + 2 * LANES) // LANES * ch + META
    whole = pl.BlockSpec(memory_space=pltpu.VMEM)
    in_specs = [pl.BlockSpec((1, ch, width), lambda i, o: (o[tile_at + i], 0, 0))]
    in_specs += [whole if first else pl.BlockSpec(memory_space=pl.ANY)] + [whole] * (len(operands) - 1)
    results = pl.pallas_call(
        functools.partial(refine_kernel, side=side, bands=bands, first=first),
        out_shape=[jax.ShapeDtypeStruct((2 * bands, rows, LANES), BF16)] + flipped,
        grid_spec=pltpu.PrefetchScalarGridSpec(
            num_scalar_prefetch=1,
            grid=(steps,),
            in_specs=in_specs,
            out_specs=[pl.BlockSpec((bands, rows, LANES), lambda i, o: (o[slot_at + i], 0, 0))]
            + [whole] * len(flipped),
            scratch_shapes=[
                pltpu.VMEM((taps, cells), BF16),
                pltpu.VMEM((hid, cells), F32),
                pltpu.VMEM((3 * hid, cells + 2 * LANES), BF16),
                pltpu.VMEM((3 * hid, cells + LANES), BF16),
                pltpu.VMEM((taps, cells), F32),
                pltpu.VMEM((ch, cells + 2 * LANES), BF16),
                pltpu.VMEM((3 * hid, cells), BF16),
                pltpu.VMEM((hid, cells), BF16),
                pltpu.VMEM((mlp, cells), BF16),
                pltpu.VMEM((hid, cells), F32),
            ],
        ),
        input_output_aliases={2: 0} if keep else {},
        compiler_params=pltpu.CompilerParams(vmem_limit_bytes=VMEM_LIMIT),
        cost_estimate=pl.CostEstimate(
            flops=steps * 4 * 10**9, bytes_accessed=steps * 2**21, transcendentals=steps * 3 * 10**6
        ),
        name=name,
    )(place, tiles, *operands)
    return (results[0], [w_out, *results[1:]]) if first else results[0]


def decode_kernel(
    place_ref, near_ref, far_ref, t_in, t_mid, out_ref, strip, act, rows_out,
    *, dev_at, lanes_in_strip, side,
):
    frames, _, _, cols = strip.shape
    frames -= 2
    frame = pl.program_id(0)
    band = out_ref.shape[2]
    dec = out_ref.shape[1]
    tall = band + 4
    ch = t_in.shape[1] // 27
    columns = lanes_in_strip
    sets = [
        [ref.at[k + d] for d in range(columns)]
        for ref in (near_ref, far_ref)
        for k in range(0, ref.shape[0], columns)
    ]
    groups = len(sets)
    lane = lane_iota(LANES)
    low = lane < side
    col = lane_iota(cols)

    @pl.when(frame == 0)
    def _():
        strip[0:2] = jnp.zeros((2,) + strip.shape[1:], BF16)
        note_at = tall * side // LANES * ch
        notes = [
            [sets[g][d][note_at : note_at + 1, :].astype(F32) for d in range(columns)]
            for g in range(groups)
        ]
        for f in range(frames):
            picks = [
                [jnp.where(notes[g][d] == f, 1.0, 0.0) for d in range(columns)]
                for g in range(groups)
            ]
            for j in range(tall // 2):
                both = []
                for d in range(columns):
                    both.append(
                        sum(
                            sets[g][d][j * ch : (j + 1) * ch, :].astype(F32)
                            * picks[g][d]
                            for g in range(groups)
                        )
                    )
                turned = [pltpu.roll(x, side, 1) for x in both]
                first = [
                    jnp.where(low, both[d], turned[d + 1]) for d in range(0, columns, 2)
                ]
                second = [
                    jnp.where(low, turned[d], both[d + 1]) for d in range(0, columns, 2)
                ]
                for y, parts in ((2 * j, first), (2 * j + 1, second)):
                    line = jnp.concatenate(parts, axis=1)
                    left = jnp.where(col > 0, pltpu.roll(line, 1, 1), 0.0)
                    right = jnp.where(col < cols - 1, pltpu.roll(line, cols - 1, 1), 0.0)
                    strip[f + 2, y] = jnp.concatenate([left, line, right], axis=0).astype(BF16)

    first_row = place_ref[dev_at] == 0
    last_row = place_ref[dev_at] == cols // side - 1

    def act_row(y):
        around = jnp.concatenate(
            [
                strip[pl.ds(frame + dt, 1), pl.ds(y + dy, 1)].reshape(3 * ch, cols)
                for dt in range(3)
                for dy in range(3)
            ],
            axis=0,
        )
        value = silu(dot(t_in[...], around))
        if y == 0:
            value = jnp.where(first_row, 0.0, value)
        if y == band + 1:
            value = jnp.where(last_row, 0.0, value)
        top = y * 3 * dec
        act[top + dec : top + 2 * dec, :] = value.astype(BF16)

    def side_rows(y):
        top = y * 3 * dec
        value = act[top + dec : top + 2 * dec, :]
        act[top : top + dec, :] = jnp.where(col > 0, pltpu.roll(value, 1, 1), 0)
        act[top + 2 * dec : top + 3 * dec, :] = jnp.where(
            col < cols - 1, pltpu.roll(value, cols - 1, 1), 0
        )

    def out_row(y):
        top = y * 3 * dec
        value = dot(t_mid[...], act[top : top + 9 * dec, :])
        value = value + act[top + 4 * dec : top + 5 * dec, :].astype(F32)
        for k in range(cols // LANES):
            rows_out[pl.ds(k * dec * band + y, dec, stride=band), :] = value[
                :, k * LANES : (k + 1) * LANES
            ]

    for y in range(band + 2):
        act_row(y)
    for y in range(band + 2):
        side_rows(y)
    for y in range(band):
        out_row(y)
    for k in range(cols // LANES):
        done = rows_out[k * dec * band : (k + 1) * dec * band, :]
        out_ref[0, :, :, k * LANES : (k + 1) * LANES] = done.reshape(dec, band, LANES).astype(BF16)


def flip_kernel(w_in, w_mid, t_in, t_mid):
    t_in[...] = w_in[...].astype(F32).T.astype(BF16)
    t_mid[...] = w_mid[...].astype(F32).T.astype(BF16)


def flip_weights(dec_in, dec_mid):
    dec = dec_in.shape[-1]
    both = (dec_in.reshape(-1, dec), dec_mid.reshape(-1, dec))
    return pl.pallas_call(
        flip_kernel,
        out_shape=[jax.ShapeDtypeStruct(w.shape[::-1], BF16) for w in both],
        in_specs=[pl.BlockSpec(memory_space=pltpu.VMEM)] * 2,
        out_specs=[pl.BlockSpec(memory_space=pltpu.VMEM)] * 2,
        cost_estimate=pl.CostEstimate(flops=10**6, bytes_accessed=2**21, transcendentals=0),
        name="flip",
    )(*both)


def decode_band(place, dev_at, near, far, t_in, t_mid, frames, columns, side):
    dec = t_in.shape[0]
    ch = t_in.shape[1] // 27
    rows = near.shape[1]
    band = (rows - META) // ch * LANES // side - 4
    cols = columns * side
    whole = pl.BlockSpec(memory_space=pltpu.VMEM)
    return pl.pallas_call(
        functools.partial(decode_kernel, dev_at=dev_at, lanes_in_strip=columns, side=side),
        out_shape=jax.ShapeDtypeStruct((frames, dec, band, cols), BF16),
        grid_spec=pltpu.PrefetchScalarGridSpec(
            num_scalar_prefetch=1,
            grid=(frames,),
            in_specs=[whole] * 4,
            out_specs=pl.BlockSpec((1, dec, band, cols), lambda f, w: (f, 0, 0, 0)),
            scratch_shapes=[
                pltpu.VMEM((frames + 2, band + 4, 3 * ch, cols), BF16),
                pltpu.VMEM(((band + 2) * 3 * dec, cols), BF16),
                pltpu.VMEM((cols // LANES * dec * band, LANES), F32),
            ],
        ),
        compiler_params=pltpu.CompilerParams(vmem_limit_bytes=VMEM_LIMIT),
        name="decode",
    )(place, near, far, t_in, t_mid)


def shards(latent, tile_routes, w_in, w_qkv, w_proj, w_mid, w_up, w_down, w_out, dec_in, dec_mid):
    halves = lax.axis_size("far")
    pairs = lax.axis_size("near")
    columns = lax.axis_size("dev")
    assert halves == 2 and pairs == 2
    own_tiles = latent[0]
    frames, ch, cells = own_tiles.shape
    side = math.isqrt(cells)
    outgoing = pick_tiles(tile_routes.reshape(-1), own_tiles, halves * pairs)
    landing = lax.all_to_all(outgoing, ("far", "near"), split_axis=0, concat_axis=0, tiled=True)
    weights = (w_in[0], w_qkv[0], w_proj[0], w_mid[0], w_up[0], w_down[0], w_out[0])
    slot = lax.axis_index("near")
    own = lax.axis_index("far") * 2 + slot
    k = jnp.arange(8, dtype=jnp.int32)
    place = jnp.where(
        k < 4,
        own ^ jnp.where(k == 0, 0, jnp.where(k == 3, 1, k + 1)),
        jnp.where(k == 6, lax.axis_index("dev"), slot ^ (k & 1)),
    )
    near, ready = refine_tiles("refine_own", place, outgoing, 1, 0, 4, weights, columns)
    far = refine_tiles("refine_far", place, landing, 2, 1, 4, None, columns, (near, False, ready))
    far_pieces = lax.all_to_all(far, ("near", "dev"), split_axis=0, concat_axis=0, tiled=True)
    near, _ = lax.optimization_barrier((near, far))
    near = refine_tiles("refine_near", place, landing, 1, 3, 5, None, columns, (near, True, ready))
    near_pieces = lax.all_to_all(near, ("near", "dev"), split_axis=0, concat_axis=0, tiled=True)
    far_pieces = lax.ppermute(far_pieces, "far", [(0, 1), (1, 0)])
    return decode_band(
        place, 6, near_pieces, far_pieces, *flip_weights(dec_in, dec_mid), frames, columns, side
    )[None]


def solution(mesh):
    devices = mesh.devices
    mesh = jax.sharding.Mesh(
        devices.reshape(2, devices.shape[0] // 2, devices.shape[1]), (*POOL, "dev")
    )
    in_specs = (
        P(POOL, None, None, "dev"),
        P(POOL, "dev", None, None),
        P(POOL, None, None, None, None),
        P(POOL, None, None),
        P(POOL, None, None),
        P(POOL, None, None, None, None),
        P(POOL, None, None),
        P(POOL, None, None),
        P(POOL, None, None, None, None),
        P(),
        P(),
    )
    out_specs = P(POOL, None, None, "dev", None)
    return jax.shard_map(shards, mesh=mesh, in_specs=in_specs, out_specs=out_specs, check_vma=False)
```

```python
import functools
import math

import jax
import jax.numpy as jnp
from jax import lax
from jax.experimental import pallas as pl
from jax.experimental.pallas import tpu as pltpu
from jax.sharding import PartitionSpec as P

HEAD = 64
WIN = 8
LANES = 128
META = 8
POOL = ("far", "near")
EPS = 1e-06
F32 = jnp.float32
BF16 = jnp.bfloat16
VMEM_LIMIT = 60 * 2**20


def dot(a, b):
    return jnp.dot(a, b, preferred_element_type=F32)


def dot_tn(a, b):
    return lax.dot_general(a, b, (((0,), (0,)), ((), ())), preferred_element_type=F32)


def silu_twice(half):
    return half + half * jnp.tanh(half)


def norm_channels(x):
    mean = jnp.mean(x * x, axis=0, keepdims=True)
    return x * lax.rsqrt(mean + EPS)


def lane_iota(width):
    return lax.broadcasted_iota(jnp.int32, (1, width), 1)


def pick_kernel(routes_ref, tile_ref, out_ref):
    groups, ch, width = out_ref.shape
    frames, _, cells = tile_ref.shape
    rows = lax.broadcasted_iota(jnp.int32, (ch, LANES), 0)
    for group in range(groups):
        named = functools.reduce(
            jnp.logical_or, [routes_ref[f] == group for f in range(frames)]
        )
        wanted = jnp.where(named, group, groups)
        frame = sum(jnp.where(routes_ref[f] == wanted, f, 0) for f in range(frames))
        out_ref[group, :, :cells] = tile_ref[frame]
        live = jnp.where(named, 1, 0)
        out_ref[group, :, cells:] = jnp.where(rows < META, frame, live).astype(F32).astype(BF16)


def pick_tiles(routes, own_tiles, groups):
    frames, ch, cells = own_tiles.shape
    assert frames == groups
    whole = pl.BlockSpec(memory_space=pltpu.VMEM)
    return pl.pallas_call(
        pick_kernel,
        out_shape=jax.ShapeDtypeStruct((groups, ch, cells + LANES), BF16),
        in_specs=[pl.BlockSpec(memory_space=pltpu.SMEM), whole],
        out_specs=whole,
        name="pick",
    )(routes, own_tiles)


def refine_kernel(*refs, side, bands, first):
    if first:
        _, tile_ref, w_in, w_qkv, w_proj, w_mid, w_up, w_down, w_out = refs[:9]
        out_ref, t_in, t_qkv, t_proj, t_mid, t_up, t_down, perm = refs[9:17]
        scratch = refs[17:]
    else:
        _, tile_ref, _, w_out, t_in, t_qkv, t_proj, t_mid, t_up, t_down, perm = refs[:11]
        out_ref = refs[11]
        scratch = refs[12:]
    patch, att, even, odd, taps, padded, qkv_ref, mixed_ref, wide, wide_f = scratch
    ch = tile_ref.shape[1]
    cells = side * side
    hid = t_proj.shape[0]
    chunk = WIN * side
    chunks = cells // chunk
    heads = hid // HEAD
    win_cells = WIN * WIN
    pair = LANES // win_cells
    assert side == WIN * WIN and pair == 2 and 2 * side == LANES

    if first:
        for flipped, weight, factor in (
            (t_in, w_in, 1.0), (t_qkv, w_qkv, 1.0), (t_proj, w_proj, 1.0),
            (t_mid, w_mid, 0.5), (t_up, w_up, 0.5), (t_down, w_down, 1.0),
        ):
            flipped[...] = (weight[...].astype(F32) * factor).T.astype(BF16)
        src = lax.broadcasted_iota(jnp.int32, (chunk, chunk), 0)
        dst = lax.broadcasted_iota(jnp.int32, (chunk, chunk), 1)
        want = ((dst >> 3) & 7) * side + (dst >> 6) * WIN + (dst & 7)
        perm[...] = jnp.where(src == want, 1.0, 0.0).astype(BF16)

    @pl.when(pl.program_id(0) == 0)
    def _():
        even[:, :LANES] = jnp.zeros((3 * hid, LANES), BF16)
        even[:, LANES + cells :] = jnp.zeros((3 * hid, LANES), BF16)
        padded[:, :LANES] = jnp.zeros((ch, LANES), BF16)
        padded[:, LANES + cells :] = jnp.zeros((ch, LANES), BF16)

    tile = tile_ref[0, :, :cells].astype(F32)
    lane = lane_iota(cells)
    row = lane >> 6
    col = lane & (side - 1)

    def inside(dy, dx):
        ok = None
        for pos, off in ((row, dy), (col, dx)):
            if off:
                good = (pos > 0) if off < 0 else (pos < side - 1)
                ok = good if ok is None else ok & good
        return ok

    def moved(x, dy, dx):
        off = dy * side + dx
        if off == 0:
            return x
        x = pltpu.roll(x, (-off) % cells, 1)
        return jnp.where(inside(dy, dx), x, 0.0)

    offsets = [(dy, dx) for dy in (-1, 0, 1) for dx in (-1, 0, 1)]
    for t, (dy, dx) in enumerate(offsets):
        patch[t * ch : (t + 1) * ch, :] = moved(tile, dy, dx).astype(BF16)

    low = lane_iota(LANES) < win_cells
    ccol = lane_iota(chunk) & (side - 1)
    scale = math.log2(math.e) / math.sqrt(HEAD)

    def lift(base):
        lifted = dot(t_in[...], patch[:, pl.ds(base, chunk)])
        att[:, pl.ds(base, chunk)] = lifted
        mixed_ref[:, pl.ds(base, chunk)] = norm_channels(lifted).astype(BF16)

    def lift2(base):
        mixed_ref[:, pl.ds(base, chunk)] = dot(mixed_ref[:, pl.ds(base, chunk)], perm[...]).astype(BF16)

    def lift3(base):
        qkv_ref[:, pl.ds(base, chunk)] = dot(t_qkv[...], mixed_ref[:, pl.ds(base, chunk)]).astype(BF16)

    head_of = lax.broadcasted_iota(jnp.int32, (1, hid), 1) < HEAD
    zero = jnp.zeros((HEAD, LANES), BF16)

    def attend(base):
        for p in range(chunk // LANES):
            at = pl.ds(base + p * LANES, LANES)
            keys = qkv_ref[hid : 2 * hid, at].T
            both = jnp.concatenate(
                [jnp.where(head_of, keys, 0), jnp.where(head_of, 0, keys)], axis=0
            ).astype(BF16)
            full = dot(both, qkv_ref[:hid, at])
            for h in range(heads):
                top = h * LANES
                wide_f[h * win_cells : (h + 1) * win_cells, at] = jnp.where(
                    low, full[top : top + win_cells], full[top + win_cells : top + LANES]
                )

    def attend2(base):
        for p in range(chunk // LANES):
            at = pl.ds(base + p * LANES, LANES)
            for h in range(heads):
                own = wide_f[h * win_cells : (h + 1) * win_cells, at]
                most = jnp.max(own, axis=0, keepdims=True)
                raised = jnp.exp2((own - most) * scale)
                total = jnp.sum(raised, axis=0, keepdims=True)
                probs = (raised * (1.0 / total)).astype(BF16)
                top = h * LANES
                wide[top : top + win_cells, at] = jnp.where(low, probs, 0)
                wide[top + win_cells : top + LANES, at] = jnp.where(low, 0, probs)

    def attend3(base):
        for p in range(chunk // LANES):
            at = pl.ds(base + p * LANES, LANES)
            values = jnp.concatenate(
                [
                    jnp.concatenate([qkv_ref[2 * hid : 2 * hid + HEAD, at], zero], axis=1),
                    jnp.concatenate([zero, qkv_ref[2 * hid + HEAD :, at]], axis=1),
                ],
                axis=0,
            )
            mixed_ref[:, at] = dot(values, wide[: heads * LANES, at]).astype(BF16)

    def project(base):
        mixed_ref[:, pl.ds(base, chunk)] = dot(mixed_ref[:, pl.ds(base, chunk)], perm[...]).astype(BF16)

    def project2(base):
        attended = att[:, pl.ds(base, chunk)] + dot(t_proj[...], mixed_ref[:, pl.ds(base, chunk)])
        att[:, pl.ds(base, chunk)] = attended
        here = pl.ds(base + LANES, chunk)
        even[hid : 2 * hid, here] = norm_channels(attended).astype(BF16)

    def project3(base):
        here = pl.ds(base + LANES, chunk)
        conv_in = even[hid : 2 * hid, here]
        even[:hid, here] = jnp.where(ccol > 0, pltpu.roll(conv_in, 1, 1), 0)
        even[2 * hid :, here] = jnp.where(ccol < side - 1, pltpu.roll(conv_in, chunk - 1, 1), 0)

    def shift(base):
        around = even[:, pl.ds(base, chunk + LANES)]
        odd[:, pl.ds(base, chunk)] = around[:, side : side + chunk]

    def finish1(base):
        after = pl.ds(base + LANES, chunk)
        around = jnp.concatenate(
            [odd[:, pl.ds(base, chunk)], even[:, after], odd[:, after]], axis=0
        )
        convolved = att[:, pl.ds(base, chunk)] + silu_twice(dot(t_mid[...], around))
        att[:, pl.ds(base, chunk)] = convolved
        mixed_ref[:, pl.ds(base, chunk)] = norm_channels(convolved).astype(BF16)

    def finish2(base):
        wide[:, pl.ds(base, chunk)] = silu_twice(dot(t_up[...], mixed_ref[:, pl.ds(base, chunk)])).astype(BF16)

    def finish3(base):
        finished = att[:, pl.ds(base, chunk)] + dot(t_down[...], wide[:, pl.ds(base, chunk)])
        mixed_ref[:, pl.ds(base, chunk)] = finished.astype(BF16)

    def finish4(base):
        taps[:, pl.ds(base, chunk)] = dot(w_out[...], mixed_ref[:, pl.ds(base, chunk)])

    lags = (
        (finish4, 14), (finish3, 13), (finish2, 12), (finish1, 11), (shift, 9), (project3, 8),
        (project2, 7), (project, 6), (attend3, 5), (attend2, 4), (attend, 3), (lift3, 2), (lift2, 1), (lift, 0),
    )
    for step in range(chunks + 14):
        for body, lag in lags:
            if 0 <= step - lag < chunks:
                body((step - lag) * chunk)
                if body is shift and step - lag == chunks - 1:
                    odd[:, cells:] = even[:, cells : cells + 2 * LANES][:, side : side + LANES]

    delta = jnp.zeros((ch, cells), F32)
    for t, (dy, dx) in enumerate(offsets):
        delta = delta + moved(taps[t * ch : (t + 1) * ch, :], dy, dx)
    delta = delta.astype(BF16).astype(F32)
    note = tile_ref[0, :, cells:]
    live = note[META : META + 1, :1].astype(F32)
    padded[:, LANES : LANES + cells] = (tile + live * delta).astype(BF16)
    band = cells // bands
    pieces = (band + 2 * LANES) // LANES
    for b in range(bands):
        for j in range(pieces):
            at = b * band + j * LANES
            out_ref[b, j * ch : (j + 1) * ch, :] = padded[:, at : at + LANES]
        out_ref[b, pieces * ch :, :] = note[:META, :]


def refine_tiles(name, place, tiles, steps, tile_at, slot_at, weights, bands, before=None):
    _, ch, width = tiles.shape
    cells = width - LANES
    side = math.isqrt(cells)
    first = before is None
    keep = False
    if first:
        w_in, w_qkv, w_proj, w_mid, w_up, w_down, w_out = weights
        hid = w_proj.shape[0]
        w_in = w_in.reshape(-1, hid)
        w_mid = w_mid.reshape(-1, hid)
        w_out = jnp.swapaxes(w_out, 2, 3).reshape(-1, hid)
        operands = (w_in, w_qkv, w_proj, w_mid, w_up, w_down, w_out)
        chunk = WIN * side
        flipped = [jax.ShapeDtypeStruct(w.shape[::-1], BF16) for w in operands[:-1]]
        flipped.append(jax.ShapeDtypeStruct((chunk, chunk), BF16))
        mlp = w_up.shape[1]
    else:
        chunks, keep, (w_out, *rest) = before
        operands = (chunks, w_out, *rest)
        hid = w_out.shape[1]
        mlp = rest[4].shape[0]
        flipped = []
    taps = w_out.shape[0]
    rows = (cells // bands + 2 * LANES) // LANES * ch + META
    whole = pl.BlockSpec(memory_space=pltpu.VMEM)
    in_specs = [pl.BlockSpec((1, ch, width), lambda i, o: (o[tile_at + i], 0, 0))]
    in_specs += [whole if first else pl.BlockSpec(memory_space=pl.ANY)] + [whole] * (len(operands) - 1)
    results = pl.pallas_call(
        functools.partial(refine_kernel, side=side, bands=bands, first=first),
        out_shape=[jax.ShapeDtypeStruct((2 * bands, rows, LANES), BF16)] + flipped,
        grid_spec=pltpu.PrefetchScalarGridSpec(
            num_scalar_prefetch=1,
            grid=(steps,),
            in_specs=in_specs,
            out_specs=[pl.BlockSpec((bands, rows, LANES), lambda i, o: (o[slot_at + i], 0, 0))]
            + [whole] * len(flipped),
            scratch_shapes=[
                pltpu.VMEM((taps, cells), BF16),
                pltpu.VMEM((hid, cells), F32),
                pltpu.VMEM((3 * hid, cells + 2 * LANES), BF16),
                pltpu.VMEM((3 * hid, cells + LANES), BF16),
                pltpu.VMEM((taps, cells), F32),
                pltpu.VMEM((ch, cells + 2 * LANES), BF16),
                pltpu.VMEM((3 * hid, cells), BF16),
                pltpu.VMEM((hid, cells), BF16),
                pltpu.VMEM((mlp, cells), BF16),
                pltpu.VMEM((hid, cells), F32),
            ],
        ),
        input_output_aliases={2: 0} if keep else {},
        compiler_params=pltpu.CompilerParams(vmem_limit_bytes=VMEM_LIMIT),
        cost_estimate=pl.CostEstimate(
            flops=steps * 4 * 10**9, bytes_accessed=steps * 2**21, transcendentals=steps * 3 * 10**6
        ),
        name=name,
    )(place, tiles, *operands)
    return (results[0], [w_out, *results[1:]]) if first else results[0]


def decode_kernel(
    place_ref, near_ref, far_ref, t_in, t_a, t_b, t_c, t_e, out_ref, strip, act, rows_out, waves,
    *, dev_at, lanes_in_strip, side,
):
    frames, _, _, cols = strip.shape
    frames -= 2
    frame = pl.program_id(0)
    band = out_ref.shape[2]
    dec = out_ref.shape[1]
    tall = band + 4
    ch = t_in.shape[1] // 27
    columns = lanes_in_strip
    sets = [
        [ref.at[k + d] for d in range(columns)]
        for ref in (near_ref, far_ref)
        for k in range(0, ref.shape[0], columns)
    ]
    groups = len(sets)
    lane = lane_iota(LANES)
    low = lane < side
    col = lane_iota(cols)

    @pl.when(frame == 0)
    def _():
        strip[0:2] = jnp.zeros((2,) + strip.shape[1:], BF16)
        note_at = tall * side // LANES * ch
        notes = [
            [sets[g][d][note_at : note_at + 1, :].astype(F32) for d in range(columns)]
            for g in range(groups)
        ]
        for f in range(frames):
            picks = [
                [jnp.where(notes[g][d] == f, 1.0, 0.0) for d in range(columns)]
                for g in range(groups)
            ]
            for j in range(tall // 2):
                both = []
                for d in range(columns):
                    both.append(
                        sum(
                            sets[g][d][j * ch : (j + 1) * ch, :].astype(F32)
                            * picks[g][d]
                            for g in range(groups)
                        )
                    )
                turned = [pltpu.roll(x, side, 1) for x in both]
                first = [
                    jnp.where(low, both[d], turned[d + 1]) for d in range(0, columns, 2)
                ]
                second = [
                    jnp.where(low, turned[d], both[d + 1]) for d in range(0, columns, 2)
                ]
                for y, parts in ((2 * j, first), (2 * j + 1, second)):
                    line = jnp.concatenate(parts, axis=1)
                    left = jnp.where(col > 0, pltpu.roll(line, 1, 1), 0.0)
                    right = jnp.where(col < cols - 1, pltpu.roll(line, cols - 1, 1), 0.0)
                    strip[f + 2, y] = jnp.concatenate([left, line, right], axis=0).astype(BF16)

    first_row = place_ref[dev_at] == 0
    last_row = place_ref[dev_at] == cols // side - 1

    def act_row(y):
        around = jnp.concatenate(
            [
                strip[pl.ds(frame + dt, 1), pl.ds(y + dy, 1)].reshape(3 * ch, cols)
                for dt in range(3)
                for dy in range(3)
            ],
            axis=0,
        )
        value = silu_twice(dot(t_in[...], around))
        if y == 0:
            value = jnp.where(first_row, 0.0, value)
        if y == band + 1:
            value = jnp.where(last_row, 0.0, value)
        top = y * 3 * dec
        act[top + dec : top + 2 * dec, :] = value.astype(BF16)

    def side_rows(y):
        top = y * 3 * dec
        value = act[top + dec : top + 2 * dec, :]
        act[top : top + dec, :] = jnp.where(col > 0, pltpu.roll(value, 1, 1), 0)
        act[top + 2 * dec : top + 3 * dec, :] = jnp.where(
            col < cols - 1, pltpu.roll(value, cols - 1, 1), 0
        )

    lead = t_b.shape[1]

    def mix_pair(y):
        r = [act[(y + k) * 3 * dec : (y + k) * 3 * dec + lead, :] for k in range(4)]
        top = y * 2 * lead
        for k, wave in enumerate((r[0] - r[2], r[1] + r[2], r[2] - r[1], r[1] - r[3])):
            waves[top + k * lead : top + (k + 1) * lead, :] = wave

    def out_pair(y):
        def wave(k):
            top = y * 2 * lead + k * lead
            return waves[top : top + lead, :]

        def rest(row):
            return [
                act[(row + dy) * 3 * dec + lead : (row + dy + 1) * 3 * dec, :] for dy in range(3)
            ]

        first = dot(t_a[...], jnp.concatenate([wave(0)] + rest(y), axis=0))
        even_part = dot(t_b[...], wave(1))
        odd_part = dot(t_c[...], wave(2))
        last = dot(t_e[...], jnp.concatenate([wave(3)] + rest(y + 1), axis=0))
        for row, value in ((y, first + (even_part + odd_part)), (y + 1, last + (even_part - odd_part))):
            top = row * 3 * dec
            value = value + act[top + 4 * dec : top + 5 * dec, :].astype(F32)
            for k in range(cols // LANES):
                rows_out[pl.ds(k * dec * band + row, dec, stride=band), :] = value[
                    :, k * LANES : (k + 1) * LANES
                ]

    for y in range(band + 2):
        act_row(y)
    for y in range(band + 2):
        side_rows(y)
    for y in range(0, band, 2):
        mix_pair(y)
    for y in range(0, band, 2):
        out_pair(y)
    for k in range(cols // LANES):
        done = rows_out[k * dec * band : (k + 1) * dec * band, :]
        out_ref[0, :, :, k * LANES : (k + 1) * LANES] = done.reshape(dec, band, LANES).astype(BF16)


def flip_kernel(w_in, w_mid, t_in, t_a, t_b, t_c, t_e):
    t_in[...] = (w_in[...].astype(F32) * 0.5).T.astype(BF16)
    depth = w_mid.shape[0] // 3
    lead = t_b.shape[1]
    g = [w_mid[k * depth : k * depth + lead, :].astype(F32) for k in range(3)]
    rest = [w_mid[k * depth + lead : (k + 1) * depth, :].astype(F32) for k in range(3)]
    t_a[...] = jnp.concatenate([g[0]] + rest, axis=0).T.astype(BF16)
    t_b[...] = (0.5 * (g[0] + g[1] + g[2])).T.astype(BF16)
    t_c[...] = (0.5 * (g[0] - g[1] + g[2])).T.astype(BF16)
    t_e[...] = jnp.concatenate([-g[2]] + rest, axis=0).T.astype(BF16)


def flip_weights(dec_in, dec_mid):
    dec = dec_in.shape[-1]
    both = (dec_in.reshape(-1, dec), dec_mid.reshape(-1, dec))
    depth = both[1].shape[0] // 3
    lead = depth // 256 * 256
    full = 3 * depth - 2 * lead
    shapes = [(dec, n) for n in (both[0].shape[0], full, lead, lead, full)]
    return pl.pallas_call(
        flip_kernel,
        out_shape=[jax.ShapeDtypeStruct(shape, BF16) for shape in shapes],
        in_specs=[pl.BlockSpec(memory_space=pltpu.VMEM)] * 2,
        out_specs=[pl.BlockSpec(memory_space=pltpu.VMEM)] * len(shapes),
        cost_estimate=pl.CostEstimate(flops=10**6, bytes_accessed=2**21, transcendentals=0),
        name="flip",
    )(*both)


def decode_band(place, dev_at, near, far, flipped, frames, columns, side):
    dec = flipped[0].shape[0]
    ch = flipped[0].shape[1] // 27
    lead = flipped[2].shape[1]
    rows = near.shape[1]
    band = (rows - META) // ch * LANES // side - 4
    assert band % 2 == 0
    cols = columns * side
    whole = pl.BlockSpec(memory_space=pltpu.VMEM)
    return pl.pallas_call(
        functools.partial(decode_kernel, dev_at=dev_at, lanes_in_strip=columns, side=side),
        out_shape=jax.ShapeDtypeStruct((frames, dec, band, cols), BF16),
        grid_spec=pltpu.PrefetchScalarGridSpec(
            num_scalar_prefetch=1,
            grid=(frames,),
            in_specs=[whole] * (2 + len(flipped)),
            out_specs=pl.BlockSpec((1, dec, band, cols), lambda f, w: (f, 0, 0, 0)),
            scratch_shapes=[
                pltpu.VMEM((frames + 2, band + 4, 3 * ch, cols), BF16),
                pltpu.VMEM(((band + 2) * 3 * dec, cols), BF16),
                pltpu.VMEM((cols // LANES * dec * band, LANES), F32),
                pltpu.VMEM((band * 2 * lead, cols), BF16),
            ],
        ),
        compiler_params=pltpu.CompilerParams(vmem_limit_bytes=VMEM_LIMIT),
        name="decode",
    )(place, near, far, *flipped)


def shards(latent, tile_routes, w_in, w_qkv, w_proj, w_mid, w_up, w_down, w_out, dec_in, dec_mid):
    halves = lax.axis_size("far")
    pairs = lax.axis_size("near")
    columns = lax.axis_size("dev")
    assert halves == 2 and pairs == 2
    own_tiles = latent[0]
    frames, ch, cells = own_tiles.shape
    side = math.isqrt(cells)
    outgoing = pick_tiles(tile_routes.reshape(-1), own_tiles, halves * pairs)
    landing = lax.all_to_all(outgoing, ("far", "near"), split_axis=0, concat_axis=0, tiled=True)
    weights = (w_in[0], w_qkv[0], w_proj[0], w_mid[0], w_up[0], w_down[0], w_out[0])
    slot = lax.axis_index("near")
    own = lax.axis_index("far") * 2 + slot
    k = jnp.arange(8, dtype=jnp.int32)
    place = jnp.where(
        k < 4,
        own ^ jnp.where(k == 0, 0, jnp.where(k == 3, 1, k + 1)),
        jnp.where(k == 6, lax.axis_index("dev"), slot ^ (k & 1)),
    )
    near, ready = refine_tiles("refine_own", place, outgoing, 1, 0, 4, weights, columns)
    far = refine_tiles("refine_far", place, landing, 2, 1, 4, None, columns, (near, False, ready))
    far_pieces = lax.all_to_all(far, ("near", "dev"), split_axis=0, concat_axis=0, tiled=True)
    near, _ = lax.optimization_barrier((near, far))
    near = refine_tiles("refine_near", place, landing, 1, 3, 5, None, columns, (near, True, ready))
    near_pieces = lax.all_to_all(near, ("near", "dev"), split_axis=0, concat_axis=0, tiled=True)
    far_pieces = lax.ppermute(far_pieces, "far", [(0, 1), (1, 0)])
    return decode_band(
        place, 6, near_pieces, far_pieces, flip_weights(dec_in, dec_mid), frames, columns, side
    )[None]


def solution(mesh):
    devices = mesh.devices
    mesh = jax.sharding.Mesh(
        devices.reshape(2, devices.shape[0] // 2, devices.shape[1]), (*POOL, "dev")
    )
    in_specs = (
        P(POOL, None, None, "dev"),
        P(POOL, "dev", None, None),
        P(POOL, None, None, None, None),
        P(POOL, None, None),
        P(POOL, None, None),
        P(POOL, None, None, None, None),
        P(POOL, None, None),
        P(POOL, None, None),
        P(POOL, None, None, None, None),
        P(),
        P(),
    )
    out_specs = P(POOL, None, None, "dev", None)
    return jax.shard_map(shards, mesh=mesh, in_specs=in_specs, out_specs=out_specs, check_vma=False)
```

```python
import functools
import math

import jax
import jax.numpy as jnp
from jax import lax
from jax.experimental import pallas as pl
from jax.experimental.pallas import tpu as pltpu
from jax.sharding import PartitionSpec as P

HEAD = 64
WIN = 8
LANES = 128
META = 8
POOL = ("far", "near")
EPS = 1e-06
F32 = jnp.float32
BF16 = jnp.bfloat16
VMEM_LIMIT = 60 * 2**20


def dot(a, b):
    return jnp.dot(a, b, preferred_element_type=F32)


def dot_tn(a, b):
    return lax.dot_general(a, b, (((0,), (0,)), ((), ())), preferred_element_type=F32)


def silu_twice(half):
    return half + half * jnp.tanh(half)


def norm_channels(x):
    mean = jnp.mean(x * x, axis=0, keepdims=True)
    return x * lax.rsqrt(mean + EPS)


def lane_iota(width):
    return lax.broadcasted_iota(jnp.int32, (1, width), 1)


def pick_kernel(routes_ref, tile_ref, out_ref):
    groups, ch, width = out_ref.shape
    frames, _, cells = tile_ref.shape
    rows = lax.broadcasted_iota(jnp.int32, (ch, LANES), 0)
    for group in range(groups):
        named = functools.reduce(
            jnp.logical_or, [routes_ref[f] == group for f in range(frames)]
        )
        wanted = jnp.where(named, group, groups)
        frame = sum(jnp.where(routes_ref[f] == wanted, f, 0) for f in range(frames))
        out_ref[group, :, :cells] = tile_ref[frame]
        live = jnp.where(named, 1, 0)
        out_ref[group, :, cells:] = jnp.where(rows < META, frame, live).astype(F32).astype(BF16)


def pick_tiles(routes, own_tiles, groups):
    frames, ch, cells = own_tiles.shape
    assert frames == groups
    whole = pl.BlockSpec(memory_space=pltpu.VMEM)
    return pl.pallas_call(
        pick_kernel,
        out_shape=jax.ShapeDtypeStruct((groups, ch, cells + LANES), BF16),
        in_specs=[pl.BlockSpec(memory_space=pltpu.SMEM), whole],
        out_specs=whole,
        name="pick",
    )(routes, own_tiles)


def refine_kernel(*refs, side, bands, first):
    if first:
        _, tile_ref, w_in, w_qkv, w_proj, w_mid, w_up, w_down, w_out = refs[:9]
        out_ref, t_in, t_qkv, t_proj, t_mid, t_up, t_down, perm = refs[9:17]
        scratch = refs[17:]
    else:
        _, tile_ref, _, w_out, t_in, t_qkv, t_proj, t_mid, t_up, t_down, perm = refs[:11]
        out_ref = refs[11]
        scratch = refs[12:]
    patch, att, even, odd, taps, padded, qkv_ref, mixed_ref, wide, wide_f = scratch
    ch = tile_ref.shape[1]
    cells = side * side
    hid = t_proj.shape[0]
    chunk = WIN * side
    chunks = cells // chunk
    heads = hid // HEAD
    win_cells = WIN * WIN
    pair = LANES // win_cells
    assert side == WIN * WIN and pair == 2 and 2 * side == LANES

    if first:
        for flipped, weight, factor in (
            (t_in, w_in, 1.0), (t_qkv, w_qkv, 1.0), (t_proj, w_proj, 1.0),
            (t_mid, w_mid, 0.5), (t_up, w_up, 0.5), (t_down, w_down, 1.0),
        ):
            flipped[...] = (weight[...].astype(F32) * factor).T.astype(BF16)
        src = lax.broadcasted_iota(jnp.int32, (chunk, chunk), 0)
        dst = lax.broadcasted_iota(jnp.int32, (chunk, chunk), 1)
        want = ((dst >> 3) & 7) * side + (dst >> 6) * WIN + (dst & 7)
        perm[...] = jnp.where(src == want, 1.0, 0.0).astype(BF16)

    @pl.when(pl.program_id(0) == 0)
    def _():
        even[:, :LANES] = jnp.zeros((3 * hid, LANES), BF16)
        even[:, LANES + cells :] = jnp.zeros((3 * hid, LANES), BF16)
        padded[:, :LANES] = jnp.zeros((ch, LANES), BF16)
        padded[:, LANES + cells :] = jnp.zeros((ch, LANES), BF16)

    tile = tile_ref[0, :, :cells].astype(F32)
    lane = lane_iota(cells)
    row = lane >> 6
    col = lane & (side - 1)

    def inside(dy, dx):
        ok = None
        for pos, off in ((row, dy), (col, dx)):
            if off:
                good = (pos > 0) if off < 0 else (pos < side - 1)
                ok = good if ok is None else ok & good
        return ok

    def moved(x, dy, dx):
        off = dy * side + dx
        if off == 0:
            return x
        x = pltpu.roll(x, (-off) % cells, 1)
        return jnp.where(inside(dy, dx), x, 0.0)

    offsets = [(dy, dx) for dy in (-1, 0, 1) for dx in (-1, 0, 1)]
    for t, (dy, dx) in enumerate(offsets):
        patch[t * ch : (t + 1) * ch, :] = moved(tile, dy, dx).astype(BF16)

    low = lane_iota(LANES) < win_cells
    ccol = lane_iota(chunk) & (side - 1)
    scale = math.log2(math.e) / math.sqrt(HEAD)

    def lift(base):
        lifted = dot(t_in[...], patch[:, pl.ds(base, chunk)])
        att[:, pl.ds(base, chunk)] = lifted
        mixed_ref[:, pl.ds(base, chunk)] = norm_channels(lifted).astype(BF16)

    def lift2(base):
        mixed_ref[:, pl.ds(base, chunk)] = dot(mixed_ref[:, pl.ds(base, chunk)], perm[...]).astype(BF16)

    def lift3(base):
        qkv_ref[:, pl.ds(base, chunk)] = dot(t_qkv[...], mixed_ref[:, pl.ds(base, chunk)]).astype(BF16)

    head_of = lax.broadcasted_iota(jnp.int32, (1, hid), 1) < HEAD
    zero = jnp.zeros((HEAD, LANES), BF16)

    def attend(base):
        for p in range(chunk // LANES):
            at = pl.ds(base + p * LANES, LANES)
            keys = qkv_ref[hid : 2 * hid, at].T
            both = jnp.concatenate(
                [jnp.where(head_of, keys, 0), jnp.where(head_of, 0, keys)], axis=0
            ).astype(BF16)
            full = dot(both, qkv_ref[:hid, at])
            for h in range(heads):
                top = h * LANES
                wide_f[h * win_cells : (h + 1) * win_cells, at] = jnp.where(
                    low, full[top : top + win_cells], full[top + win_cells : top + LANES]
                )

    def attend2(base):
        for p in range(chunk // LANES):
            at = pl.ds(base + p * LANES, LANES)
            for h in range(heads):
                own = wide_f[h * win_cells : (h + 1) * win_cells, at]
                most = jnp.max(own, axis=0, keepdims=True)
                raised = jnp.exp2((own - most) * scale)
                total = jnp.sum(raised, axis=0, keepdims=True)
                probs = (raised * (1.0 / total)).astype(BF16)
                top = h * LANES
                wide[top : top + win_cells, at] = jnp.where(low, probs, 0)
                wide[top + win_cells : top + LANES, at] = jnp.where(low, 0, probs)

    def attend3(base):
        for p in range(chunk // LANES):
            at = pl.ds(base + p * LANES, LANES)
            values = jnp.concatenate(
                [
                    jnp.concatenate([qkv_ref[2 * hid : 2 * hid + HEAD, at], zero], axis=1),
                    jnp.concatenate([zero, qkv_ref[2 * hid + HEAD :, at]], axis=1),
                ],
                axis=0,
            )
            mixed_ref[:, at] = dot(values, wide[: heads * LANES, at]).astype(BF16)

    def project(base):
        mixed_ref[:, pl.ds(base, chunk)] = dot(mixed_ref[:, pl.ds(base, chunk)], perm[...]).astype(BF16)

    def project2(base):
        attended = att[:, pl.ds(base, chunk)] + dot(t_proj[...], mixed_ref[:, pl.ds(base, chunk)])
        att[:, pl.ds(base, chunk)] = attended
        here = pl.ds(base + LANES, chunk)
        even[hid : 2 * hid, here] = norm_channels(attended).astype(BF16)

    def project3(base):
        here = pl.ds(base + LANES, chunk)
        conv_in = even[hid : 2 * hid, here]
        even[:hid, here] = jnp.where(ccol > 0, pltpu.roll(conv_in, 1, 1), 0)
        even[2 * hid :, here] = jnp.where(ccol < side - 1, pltpu.roll(conv_in, chunk - 1, 1), 0)

    def shift(base):
        around = even[:, pl.ds(base, chunk + LANES)]
        odd[:, pl.ds(base, chunk)] = around[:, side : side + chunk]

    def finish1(base):
        after = pl.ds(base + LANES, chunk)
        around = jnp.concatenate(
            [odd[:, pl.ds(base, chunk)], even[:, after], odd[:, after]], axis=0
        )
        convolved = att[:, pl.ds(base, chunk)] + silu_twice(dot(t_mid[...], around))
        att[:, pl.ds(base, chunk)] = convolved
        mixed_ref[:, pl.ds(base, chunk)] = norm_channels(convolved).astype(BF16)

    def finish2(base):
        wide[:, pl.ds(base, chunk)] = silu_twice(dot(t_up[...], mixed_ref[:, pl.ds(base, chunk)])).astype(BF16)

    def finish3(base):
        finished = att[:, pl.ds(base, chunk)] + dot(t_down[...], wide[:, pl.ds(base, chunk)])
        mixed_ref[:, pl.ds(base, chunk)] = finished.astype(BF16)

    def finish4(base):
        taps[:, pl.ds(base, chunk)] = dot(w_out[...], mixed_ref[:, pl.ds(base, chunk)])

    lags = (
        (finish4, 14), (finish3, 13), (finish2, 12), (finish1, 11), (shift, 9), (project3, 8),
        (project2, 7), (project, 6), (attend3, 5), (attend2, 4), (attend, 3), (lift3, 2), (lift2, 1), (lift, 0),
    )
    for step in range(chunks + 14):
        for body, lag in lags:
            if 0 <= step - lag < chunks:
                body((step - lag) * chunk)
                if body is shift and step - lag == chunks - 1:
                    odd[:, cells:] = even[:, cells : cells + 2 * LANES][:, side : side + LANES]

    delta = jnp.zeros((ch, cells), F32)
    for t, (dy, dx) in enumerate(offsets):
        delta = delta + moved(taps[t * ch : (t + 1) * ch, :], dy, dx)
    delta = delta.astype(BF16).astype(F32)
    note = tile_ref[0, :, cells:]
    live = note[META : META + 1, :1].astype(F32)
    padded[:, LANES : LANES + cells] = (tile + live * delta).astype(BF16)
    band = cells // bands
    pieces = (band + 2 * LANES) // LANES
    for b in range(bands):
        for j in range(pieces):
            at = b * band + j * LANES
            out_ref[b, j * ch : (j + 1) * ch, :] = padded[:, at : at + LANES]
        out_ref[b, pieces * ch :, :] = note[:META, :]


def refine_tiles(name, place, tiles, steps, tile_at, slot_at, weights, bands, before=None):
    _, ch, width = tiles.shape
    cells = width - LANES
    side = math.isqrt(cells)
    first = before is None
    keep = False
    if first:
        w_in, w_qkv, w_proj, w_mid, w_up, w_down, w_out = weights
        hid = w_proj.shape[0]
        w_in = w_in.reshape(-1, hid)
        w_mid = w_mid.reshape(-1, hid)
        w_out = jnp.swapaxes(w_out, 2, 3).reshape(-1, hid)
        operands = (w_in, w_qkv, w_proj, w_mid, w_up, w_down, w_out)
        chunk = WIN * side
        flipped = [jax.ShapeDtypeStruct(w.shape[::-1], BF16) for w in operands[:-1]]
        flipped.append(jax.ShapeDtypeStruct((chunk, chunk), BF16))
        mlp = w_up.shape[1]
    else:
        chunks, keep, (w_out, *rest) = before
        operands = (chunks, w_out, *rest)
        hid = w_out.shape[1]
        mlp = rest[4].shape[0]
        flipped = []
    taps = w_out.shape[0]
    rows = (cells // bands + 2 * LANES) // LANES * ch + META
    whole = pl.BlockSpec(memory_space=pltpu.VMEM)
    in_specs = [pl.BlockSpec((1, ch, width), lambda i, o: (o[tile_at + i], 0, 0))]
    in_specs += [whole if first else pl.BlockSpec(memory_space=pl.ANY)] + [whole] * (len(operands) - 1)
    results = pl.pallas_call(
        functools.partial(refine_kernel, side=side, bands=bands, first=first),
        out_shape=[jax.ShapeDtypeStruct((2 * bands, rows, LANES), BF16)] + flipped,
        grid_spec=pltpu.PrefetchScalarGridSpec(
            num_scalar_prefetch=1,
            grid=(steps,),
            in_specs=in_specs,
            out_specs=[pl.BlockSpec((bands, rows, LANES), lambda i, o: (o[slot_at + i], 0, 0))]
            + [whole] * len(flipped),
            scratch_shapes=[
                pltpu.VMEM((taps, cells), BF16),
                pltpu.VMEM((hid, cells), F32),
                pltpu.VMEM((3 * hid, cells + 2 * LANES), BF16),
                pltpu.VMEM((3 * hid, cells + LANES), BF16),
                pltpu.VMEM((taps, cells), F32),
                pltpu.VMEM((ch, cells + 2 * LANES), BF16),
                pltpu.VMEM((3 * hid, cells), BF16),
                pltpu.VMEM((hid, cells), BF16),
                pltpu.VMEM((mlp, cells), BF16),
                pltpu.VMEM((hid, cells), F32),
            ],
        ),
        input_output_aliases={2: 0} if keep else {},
        compiler_params=pltpu.CompilerParams(vmem_limit_bytes=VMEM_LIMIT),
        cost_estimate=pl.CostEstimate(
            flops=steps * 4 * 10**9, bytes_accessed=steps * 2**21, transcendentals=steps * 3 * 10**6
        ),
        name=name,
    )(place, tiles, *operands)
    return (results[0], [w_out, *results[1:]]) if first else results[0]


def decode_kernel(
    place_ref, near_ref, far_ref, t_in, t_a, t_b, t_c, t_e, out_ref, strip, act, rows_out, waves, ahead,
    *, dev_at, lanes_in_strip, side,
):
    cols = strip.shape[3]
    frame = pl.program_id(0)
    band = out_ref.shape[2]
    dec = out_ref.shape[1]
    tall = band + 4
    ch = t_in.shape[1] // 27
    columns = lanes_in_strip
    sets = [
        [ref.at[k + d] for d in range(columns)]
        for ref in (near_ref, far_ref)
        for k in range(0, ref.shape[0], columns)
    ]
    groups = len(sets)
    lane = lane_iota(LANES)
    low = lane < side
    col = lane_iota(cols)

    def build(f, into):
        note_at = tall * side // LANES * ch
        picks = [
            [
                jnp.where(
                    sets[g][d][note_at : note_at + 1, :].astype(F32).astype(jnp.int32) == f, 1.0, 0.0
                )
                for d in range(columns)
            ]
            for g in range(groups)
        ]
        for j in range(tall // 2):
            both = [
                sum(
                    sets[g][d][j * ch : (j + 1) * ch, :].astype(F32) * picks[g][d]
                    for g in range(groups)
                )
                for d in range(columns)
            ]
            turned = [pltpu.roll(x, side, 1) for x in both]
            first = [jnp.where(low, both[d], turned[d + 1]) for d in range(0, columns, 2)]
            second = [jnp.where(low, turned[d], both[d + 1]) for d in range(0, columns, 2)]
            for y, parts in ((2 * j, first), (2 * j + 1, second)):
                line = jnp.concatenate(parts, axis=1)
                left = jnp.where(col > 0, pltpu.roll(line, 1, 1), 0.0)
                right = jnp.where(col < cols - 1, pltpu.roll(line, cols - 1, 1), 0.0)
                whole = jnp.concatenate([left, line, right], axis=0).astype(BF16)
                into(y, whole)

    @pl.when(frame == 0)
    def _():
        strip[0:2] = jnp.zeros((2,) + strip.shape[1:], BF16)

        def here(y, rows):
            strip[2, y] = rows

        build(frame, here)

    @pl.when(frame > 0)
    def _():
        strip[pl.ds(frame + 2, 1)] = ahead[...][None]

    first_row = place_ref[dev_at] == 0
    last_row = place_ref[dev_at] == cols // side - 1

    def act_row(y):
        around = jnp.concatenate(
            [
                strip[pl.ds(frame + dt, 1), pl.ds(y + dy, 1)].reshape(3 * ch, cols)
                for dt in range(3)
                for dy in range(3)
            ],
            axis=0,
        )
        value = silu_twice(dot(t_in[...], around))
        if y == 0:
            value = jnp.where(first_row, 0.0, value)
        if y == band + 1:
            value = jnp.where(last_row, 0.0, value)
        top = y * 3 * dec
        act[top + dec : top + 2 * dec, :] = value.astype(BF16)

    def side_rows(y):
        top = y * 3 * dec
        value = act[top + dec : top + 2 * dec, :]
        act[top : top + dec, :] = jnp.where(col > 0, pltpu.roll(value, 1, 1), 0)
        act[top + 2 * dec : top + 3 * dec, :] = jnp.where(
            col < cols - 1, pltpu.roll(value, cols - 1, 1), 0
        )

    lead = t_b.shape[1]

    def mix_pair(y):
        r = [act[(y + k) * 3 * dec : (y + k) * 3 * dec + lead, :] for k in range(4)]
        top = y * 2 * lead
        for k, wave in enumerate((r[0] - r[2], r[1] + r[2], r[2] - r[1], r[1] - r[3])):
            waves[top + k * lead : top + (k + 1) * lead, :] = wave

    def out_pair(y):
        def wave(k):
            top = y * 2 * lead + k * lead
            return waves[top : top + lead, :]

        def rest(row):
            return [
                act[(row + dy) * 3 * dec + lead : (row + dy + 1) * 3 * dec, :] for dy in range(3)
            ]

        first = dot(t_a[...], jnp.concatenate([wave(0)] + rest(y), axis=0))
        even_part = dot(t_b[...], wave(1))
        odd_part = dot(t_c[...], wave(2))
        last = dot(t_e[...], jnp.concatenate([wave(3)] + rest(y + 1), axis=0))
        for row, value in ((y, first + (even_part + odd_part)), (y + 1, last + (even_part - odd_part))):
            top = row * 3 * dec
            value = value + act[top + 4 * dec : top + 5 * dec, :].astype(F32)
            for k in range(cols // LANES):
                rows_out[pl.ds(k * dec * band + row, dec, stride=band), :] = value[
                    :, k * LANES : (k + 1) * LANES
                ]

    for y in range(band + 2):
        act_row(y)
    def there(y, rows):
        ahead[y] = rows

    build(frame + 1, there)
    for y in range(band + 2):
        side_rows(y)
    for y in range(0, band, 2):
        mix_pair(y)
    for y in range(0, band, 2):
        out_pair(y)
    for k in range(cols // LANES):
        done = rows_out[k * dec * band : (k + 1) * dec * band, :]
        out_ref[0, :, :, k * LANES : (k + 1) * LANES] = done.reshape(dec, band, LANES).astype(BF16)


def flip_kernel(w_in, w_mid, t_in, t_a, t_b, t_c, t_e):
    t_in[...] = (w_in[...].astype(F32) * 0.5).T.astype(BF16)
    depth = w_mid.shape[0] // 3
    lead = t_b.shape[1]
    g = [w_mid[k * depth : k * depth + lead, :].astype(F32) for k in range(3)]
    rest = [w_mid[k * depth + lead : (k + 1) * depth, :].astype(F32) for k in range(3)]
    t_a[...] = jnp.concatenate([g[0]] + rest, axis=0).T.astype(BF16)
    t_b[...] = (0.5 * (g[0] + g[1] + g[2])).T.astype(BF16)
    t_c[...] = (0.5 * (g[0] - g[1] + g[2])).T.astype(BF16)
    t_e[...] = jnp.concatenate([-g[2]] + rest, axis=0).T.astype(BF16)


def flip_weights(dec_in, dec_mid):
    dec = dec_in.shape[-1]
    both = (dec_in.reshape(-1, dec), dec_mid.reshape(-1, dec))
    depth = both[1].shape[0] // 3
    lead = depth // 256 * 256
    full = 3 * depth - 2 * lead
    shapes = [(dec, n) for n in (both[0].shape[0], full, lead, lead, full)]
    return pl.pallas_call(
        flip_kernel,
        out_shape=[jax.ShapeDtypeStruct(shape, BF16) for shape in shapes],
        in_specs=[pl.BlockSpec(memory_space=pltpu.VMEM)] * 2,
        out_specs=[pl.BlockSpec(memory_space=pltpu.VMEM)] * len(shapes),
        cost_estimate=pl.CostEstimate(flops=10**6, bytes_accessed=2**21, transcendentals=0),
        name="flip",
    )(*both)


def decode_band(place, dev_at, near, far, flipped, frames, columns, side):
    dec = flipped[0].shape[0]
    ch = flipped[0].shape[1] // 27
    lead = flipped[2].shape[1]
    rows = near.shape[1]
    band = (rows - META) // ch * LANES // side - 4
    assert band % 2 == 0
    cols = columns * side
    whole = pl.BlockSpec(memory_space=pltpu.VMEM)
    return pl.pallas_call(
        functools.partial(decode_kernel, dev_at=dev_at, lanes_in_strip=columns, side=side),
        out_shape=jax.ShapeDtypeStruct((frames, dec, band, cols), BF16),
        grid_spec=pltpu.PrefetchScalarGridSpec(
            num_scalar_prefetch=1,
            grid=(frames,),
            in_specs=[whole] * (2 + len(flipped)),
            out_specs=pl.BlockSpec((1, dec, band, cols), lambda f, w: (f, 0, 0, 0)),
            scratch_shapes=[
                pltpu.VMEM((frames + 2, band + 4, 3 * ch, cols), BF16),
                pltpu.VMEM(((band + 2) * 3 * dec, cols), BF16),
                pltpu.VMEM((cols // LANES * dec * band, LANES), F32),
                pltpu.VMEM((band * 2 * lead, cols), BF16),
                pltpu.VMEM((band + 4, 3 * ch, cols), BF16),
            ],
        ),
        compiler_params=pltpu.CompilerParams(vmem_limit_bytes=VMEM_LIMIT),
        name="decode",
    )(place, near, far, *flipped)


def shards(latent, tile_routes, w_in, w_qkv, w_proj, w_mid, w_up, w_down, w_out, dec_in, dec_mid):
    halves = lax.axis_size("far")
    pairs = lax.axis_size("near")
    columns = lax.axis_size("dev")
    assert halves == 2 and pairs == 2
    own_tiles = latent[0]
    frames, ch, cells = own_tiles.shape
    side = math.isqrt(cells)
    outgoing = pick_tiles(tile_routes.reshape(-1), own_tiles, halves * pairs)
    landing = lax.all_to_all(outgoing, ("far", "near"), split_axis=0, concat_axis=0, tiled=True)
    weights = (w_in[0], w_qkv[0], w_proj[0], w_mid[0], w_up[0], w_down[0], w_out[0])
    slot = lax.axis_index("near")
    own = lax.axis_index("far") * 2 + slot
    k = jnp.arange(8, dtype=jnp.int32)
    place = jnp.where(
        k < 4,
        own ^ jnp.where(k == 0, 0, jnp.where(k == 3, 1, k + 1)),
        jnp.where(k == 6, lax.axis_index("dev"), slot ^ (k & 1)),
    )
    near, ready = refine_tiles("refine_own", place, outgoing, 1, 0, 4, weights, columns)
    far = refine_tiles("refine_far", place, landing, 2, 1, 4, None, columns, (near, False, ready))
    far_pieces = lax.all_to_all(far, ("near", "dev"), split_axis=0, concat_axis=0, tiled=True)
    near, _ = lax.optimization_barrier((near, far))
    near = refine_tiles("refine_near", place, landing, 1, 3, 5, None, columns, (near, True, ready))
    near_pieces = lax.all_to_all(near, ("near", "dev"), split_axis=0, concat_axis=0, tiled=True)
    far_pieces = lax.ppermute(far_pieces, "far", [(0, 1), (1, 0)])
    return decode_band(
        place, 6, near_pieces, far_pieces, flip_weights(dec_in, dec_mid), frames, columns, side
    )[None]


def solution(mesh):
    devices = mesh.devices
    mesh = jax.sharding.Mesh(
        devices.reshape(2, devices.shape[0] // 2, devices.shape[1]), (*POOL, "dev")
    )
    in_specs = (
        P(POOL, None, None, "dev"),
        P(POOL, "dev", None, None),
        P(POOL, None, None, None, None),
        P(POOL, None, None),
        P(POOL, None, None),
        P(POOL, None, None, None, None),
        P(POOL, None, None),
        P(POOL, None, None),
        P(POOL, None, None, None, None),
        P(),
        P(),
    )
    out_specs = P(POOL, None, None, "dev", None)
    return jax.shard_map(shards, mesh=mesh, in_specs=in_specs, out_specs=out_specs, check_vma=False)
```
